128 devices in a mesh: grid: 16 (over z_hi, y, core), ao: 8 (over x, z_lo).
Axes of the slice: x: 4, y: 4, z: 4 (z_hi: 2, z_lo: 2; z = z_hi * 2 + z_lo), core: 2. Of those that a mesh axis runs over, the one named last changes fastest.
Arguments:
- trial: bfloat16 [12288, 16, 2, 128], P('ao'), may hold values from -0.15625 to 0.15625
- occupied: bfloat16 [12288, 2, 128], P('ao'), may hold values from -0.15625 to 0.15625
- colloc: bfloat16 [64, 128, 1536], P('grid'), may hold values from -3 to 3
- blocks: int32 [64, 12], P('grid'), may hold values from 0 to 95, as said below
- coords: float32 [64, 3, 128], P('grid'), may hold values from 0 to 4
- weights: float32 [64, 128], P('grid'), may hold values from 0.02 to 0.2
Outputs:
- exchange: float32 [16, 12288, 2, 128], P('ao', 'grid')
The draws below stay inside these ranges and needn't reach their ends.
Inputs may be any that keep to these rules, and one draw needn't show every extreme that they name: The 12 blocks of a batch are distinct and lie among 24 cyclically consecutive shell blocks.
All inputs are finite; a program needn't handle non-finite values.
Results may differ from the reference program's by a relative error of at most 0.0053.
Values may be sent and summed in bfloat16 or wider, within the bound.
A program may use at most 128 MiB of HBM per device.

```python
import math
import jax
import jax.numpy as jnp
from jax import lax

BLK = 128
NBLK = 96
NVEC = 16
NOCC = 128
P_SIZE = 128
SIG = 12
NBATCH = 64
NAO = 12288


def draw_blocks(key, part):
    centers = jax.random.randint(key, (NBATCH,), 0, NBLK)
    batch_keys = jax.random.split(jax.random.fold_in(key, 7), NBATCH)
    offsets = jax.vmap(lambda one_key: jax.random.permutation(one_key, 2 * SIG)[:SIG])(batch_keys)
    return ((centers[:, None] + offsets) % NBLK).astype(jnp.int32)


def block_levels(rng, dims, pieces, low, largest):
    def one(position, parts):
        steps = jax.random.uniform(jax.random.fold_in(jax.random.fold_in(rng, 6), position), (parts,), jnp.float32, low / len(pieces), largest / len(pieces))
        return jnp.repeat(jnp.exp(steps), dims[position] // parts).reshape((-1,) + (1,) * (len(dims) - position - 1))

    gain = one(*pieces[0])
    for cut in pieces[1:]:
        gain = gain * one(*cut)
    return gain


def normal_values(own_key, dims, deviation, bound, shards=(), held_as=jnp.bfloat16):
    gain = block_levels(own_key, dims, shards, -0.22, 0.18) if shards else 1.0
    values = jax.random.normal(own_key, dims, jnp.float32) * deviation * gain
    return jnp.minimum(jnp.maximum(values, -bound), bound).astype(held_as)


def setup_inputs(seed: int = 0) -> dict:
    streams_of = jax.random.split(jax.random.key(seed), 7)
    return {
        "trial": normal_values(streams_of[0], (NAO, NVEC, 2, NOCC), (SIG * BLK) ** -0.5, 0.15625, ((0, 8),)),
        "occupied": normal_values(streams_of[1], (NAO, 2, NOCC), (SIG * BLK) ** -0.5, 0.15625, ((0, 8),)),
        "colloc": normal_values(streams_of[2], (NBATCH, P_SIZE, SIG * BLK), 0.5, 3.0, ((0, 16),)),
        "blocks": draw_blocks(jax.random.fold_in(streams_of[6], 71), 0),
        "coords": jnp.clip(4.0 * jax.random.uniform(streams_of[4], (NBATCH, 3, P_SIZE), jnp.float32) ** block_levels(streams_of[4], (NBATCH, 3, P_SIZE), ((0, 16),), -0.2, 0.2), 0.0, 4.0),
        "weights": jnp.clip(jnp.exp(math.log(0.2) - 2.3025851 * jax.random.uniform(streams_of[5], (NBATCH, P_SIZE), jnp.float32) ** block_levels(streams_of[5], (NBATCH, P_SIZE), ((0, 16),), -0.2, 0.2)), 0.02, 0.2),
    }


def kernel_matrix(points, quad):
    differ = points[:, :, None] - points[:, None, :]
    square = lax.optimization_barrier(jnp.sum(differ * differ, axis=0))
    return quad[:, None] * quad[None, :] / jnp.sqrt(square + 0.25)

def pair_exchange(lg_half, og_half, kernel):
    lreal = lg_half[:, :, 0].astype(jnp.float32)
    limag = lg_half[:, :, 1].astype(jnp.float32)
    oreal = og_half[:, 0].astype(jnp.float32)
    oimag = og_half[:, 1].astype(jnp.float32)
    rho_real = jnp.einsum('gvi,hi->vgh', lreal, oreal) + jnp.einsum('gvi,hi->vgh', limag, oimag)
    rho_imag = jnp.einsum('gvi,hi->vgh', limag, oreal) - jnp.einsum('gvi,hi->vgh', lreal, oimag)
    m_real = (rho_real * kernel[None]).astype(jnp.bfloat16).astype(jnp.float32)
    m_imag = (rho_imag * kernel[None]).astype(jnp.bfloat16).astype(jnp.float32)
    e_real = jnp.einsum('vgh,hj->gvj', m_real, oreal) - jnp.einsum('vgh,hj->gvj', m_imag, oimag)
    e_imag = jnp.einsum('vgh,hj->gvj', m_real, oimag) + jnp.einsum('vgh,hj->gvj', m_imag, oreal)
    return jnp.stack([e_real, e_imag], axis=2).astype(jnp.bfloat16)

def reference(trial, occupied, colloc, blocks, coords, weights):
    width = NVEC * 2 * NOCC
    combined = jnp.concatenate([trial.reshape(NAO, width), occupied.reshape(NAO, 2 * NOCC)], axis=1)
    combined = combined.reshape(NBLK, BLK, width + 2 * NOCC)

    def one_batch(running, batch_items):
        values, block_ids, points, quad = batch_items
        picked = combined[block_ids].reshape(SIG * BLK, width + 2 * NOCC)
        dens = jnp.dot(values, picked, preferred_element_type=jnp.float32)
        lg_half = dens[:, :width].reshape(P_SIZE, NVEC, 2, NOCC).astype(jnp.bfloat16)
        og_half = dens[:, width:].reshape(P_SIZE, 2, NOCC).astype(jnp.bfloat16)
        potential = pair_exchange(lg_half, og_half, kernel_matrix(points, quad))
        contrib = jnp.dot(values.T, potential.reshape(P_SIZE, width), preferred_element_type=jnp.float32)
        running = running.at[block_ids].add(contrib.reshape(SIG, BLK, width))
        return (running, None)
    panel, _ = lax.scan(one_batch, jnp.zeros((NBLK, BLK, width), jnp.float32), (colloc, blocks, coords, weights))
    return panel.reshape(NAO, NVEC, 2, NOCC).transpose(1, 0, 2, 3)
```

```python
import functools
import jax
import jax.numpy as jnp
from jax import lax
from jax.experimental import pallas as pl
from jax.experimental.pallas import tpu as pltpu
from jax.sharding import PartitionSpec as P

BLK = 128
NOCC = 128
SIG = 12
F32 = jnp.float32
BF16 = jnp.bfloat16
MESH = pl.DeviceIdType.MESH
ROWS = 512


def coords_of():
    g = lax.axis_index("grid")
    a = lax.axis_index("ao")
    return g // 8, lax.rem(g // 2, 4), lax.rem(g, 2), a // 2, lax.rem(a, 2)


def device_at(zh, y, c, x, zl):
    return (zh * 8 + y * 2 + c, x * 2 + zl)


def prep_kernel(idx_ref, x_ref, occ_ref, xloc_ref, od_ref, w):
    nloc = xloc_ref.shape[1] // BLK
    for k in range(0, w.shape[0], 256):
        both = occ_ref[k : k + 256].astype(F32)
        w[k : k + 256, :NOCC] = both[:, 0, :].astype(BF16)
        w[k : k + 256, NOCC:] = both[:, 1, :].astype(BF16)
    for b in range(4):
        for l in range(nloc):
            s = idx_ref[b, l]
            at = pl.multiple_of(jnp.minimum(s, SIG - 1) * BLK, BLK)
            tile = x_ref[b, :, pl.ds(at, BLK)]
            xloc_ref[b * BLK : (b + 1) * BLK, l * BLK : (l + 1) * BLK] = jnp.where(
                s < SIG, tile, jnp.zeros_like(tile)
            )
    od_ref[...] = jnp.dot(xloc_ref[...], w[...], preferred_element_type=F32)


def prep(idx, colloc, occupied):
    rows = occupied.shape[0]
    return pl.pallas_call(
        prep_kernel,
        out_shape=(
            jax.ShapeDtypeStruct((ROWS, rows), BF16),
            jax.ShapeDtypeStruct((ROWS, 2 * NOCC), F32),
        ),
        in_specs=[
            pl.BlockSpec(memory_space=pltpu.SMEM),
            pl.BlockSpec(memory_space=pltpu.VMEM),
            pl.BlockSpec(memory_space=pltpu.VMEM),
        ],
        out_specs=(pl.BlockSpec(memory_space=pltpu.VMEM),) * 2,
        scratch_shapes=[pltpu.VMEM((rows, 2 * NOCC), BF16)],
        compiler_params=pltpu.CompilerParams(vmem_limit_bytes=40 << 20),
        name="prep",
    )(idx, colloc, occupied)


class GatherY:
    def __init__(self, own, slots, send, recv, local):
        self.own, self.slots = own, slots
        self.send, self.recv, self.local = send, recv, local
        zh, y, c, x, zl = coords_of()
        self.right = device_at(zh, lax.rem(y + 1, 4), c, x, zl)
        self.left = device_at(zh, lax.rem(y + 3, 4), c, x, zl)
        self.twin = device_at(zh, y, 1 - c, x, zl)

    def copy(self, n, src, dst, to):
        return pltpu.make_async_remote_copy(
            src_ref=src, dst_ref=dst, send_sem=self.send.at[n], recv_sem=self.recv.at[n],
            device_id=to, device_id_type=MESH,
        )

    def at(self, n):
        s, own = self.slots, self.own
        lo, hi = pl.ds(0, 2), pl.ds(2, 2)
        src, dst, to = [
            (own, s.at[0, 1], self.right),
            (own, s.at[0, 2], self.left),
            (own, s.at[1, 0], self.twin),
            (s.at[0, 1, lo], s.at[0, 3, lo], self.right),
            (s.at[0, 2, hi], s.at[0, 3, hi], self.left),
            (s.at[0, 1], s.at[1, 1], self.twin),
            (s.at[0, 2], s.at[1, 2], self.twin),
            (s.at[0, 3], s.at[1, 3], self.twin),
        ][n]
        return self.copy(n, src, dst, to)

    def keep(self):
        return pltpu.make_async_copy(self.own, self.slots.at[0, 0], self.local)

    def start(self):
        for n in (0, 1, 2):
            self.at(n).start()
        self.keep().start()

    def forward(self):
        self.at(0).wait_recv()
        self.at(3).start()
        self.at(5).start()
        self.at(1).wait_recv()
        self.at(4).start()
        self.at(6).start()

    def finish(self):
        self.at(3).wait_recv()
        self.at(4).wait_recv()
        self.at(7).start()
        for n in (2, 5, 6, 7):
            self.at(n).wait_recv()
        for n in range(8):
            self.at(n).wait_send()
        self.keep().wait()


def greet(peers):
    barrier = pltpu.get_barrier_semaphore()
    for peer in peers:
        pl.semaphore_signal(barrier, inc=1, device_id=peer, device_id_type=MESH)
    pl.semaphore_wait(barrier, len(peers))


def density_kernel(
    trial_ref, xloc_ref, x_ref, lg_ref, xall_ref,
    buf, w, opp, part, own, rec1, rec2, zsend, zrec,
    load_sem, send, recv, gsend, grecv, glocal,
):
    zh, y, c, x, zl = coords_of()
    right = device_at(zh, y, c, lax.rem(x + 1, 4), zl)
    left = device_at(zh, y, c, lax.rem(x + 3, 4), zl)
    across = device_at(zh, y, c, x, 1 - zl)
    order = [lax.rem(x + d, 4) for d in (2, 1, 3, 0)]
    gather = GatherY(x_ref, xall_ref, gsend, grecv, glocal)

    def load(v):
        return pltpu.make_async_copy(trial_ref.at[:, v], buf.at[v], load_sem.at[v])

    for dest in order:
        for t in range(4):
            load(dest * 4 + t).start()

    greet([right, left, across, gather.right, gather.left, gather.twin])
    gather.start()

    def densities(dest, store):
        def one(t, _):
            v = dest * 4 + t
            load(v).wait()

            def split(k, _):
                k = pl.multiple_of(k * 256, 256)
                both = buf[v, pl.ds(k, 256)].astype(F32)
                w[pl.ds(k, 256), :NOCC] = both[:, 0, :].astype(BF16)
                w[pl.ds(k, 256), NOCC:] = both[:, 1, :].astype(BF16)
                return 0

            lax.fori_loop(0, w.shape[0] // 256, split, 0)
            store(
                pl.ds(pl.multiple_of(t * 256, 256), 256),
                jnp.dot(xloc_ref[...], w[...], preferred_element_type=F32),
            )
            return 0

        lax.fori_loop(0, 4, one, 0)

    def remote(n, src, dst, to):
        return pltpu.make_async_remote_copy(
            src_ref=src, dst_ref=dst, send_sem=send.at[n], recv_sem=recv.at[n],
            device_id=to, device_id_type=MESH,
        )

    lo, hi = pl.ds(0, 256), pl.ds(256, 256)
    copies = [
        remote(0, opp.at[lo], rec1.at[0], right),
        remote(1, opp.at[hi], rec1.at[1], left),
        remote(2, part.at[0, hi], rec2.at[0, hi], right),
        remote(3, part.at[1, lo], rec2.at[1, lo], left),
        remote(4, part.at[0, lo], rec2.at[0, lo], right),
        remote(5, part.at[1, hi], rec2.at[1, hi], left),
        remote(6, zsend, zrec, across),
    ]

    def store_opp(cols, value):
        opp[:, cols] = value.astype(BF16)

    def store_right(cols, value):
        own[lo, cols] = value[:256]
        part[0, hi, cols] = value[256:].astype(BF16)

    def store_left(cols, value):
        part[1, lo, cols] = value[:256].astype(BF16)
        own[hi, cols] = value[256:]

    def store_own(cols, value):
        own[:, cols] = value

    densities(order[0], store_opp)
    copies[0].start()
    copies[1].start()
    densities(order[1], store_right)
    copies[2].start()
    copies[0].wait_recv()

    def add_right(i, _):
        r = pl.ds(pl.multiple_of(i * 16, 16), 16)
        part[0, r] = (own[r] + rec1[0, r].astype(F32)).astype(BF16)
        return 0

    lax.fori_loop(0, 16, add_right, 0)
    copies[4].start()
    densities(order[2], store_left)
    copies[3].start()
    copies[1].wait_recv()

    def add_left(i, _):
        r = pl.ds(pl.multiple_of(i * 16, 16), 16)
        q = pl.ds(pl.multiple_of(256 + i * 16, 16), 16)
        part[1, q] = (own[q] + rec1[1, r].astype(F32)).astype(BF16)
        return 0

    lax.fori_loop(0, 16, add_left, 0)
    copies[5].start()
    densities(order[3], store_own)
    gather.forward()
    for n in (2, 3, 4, 5):
        copies[n].wait_recv()

    theirs = pl.ds(pl.multiple_of((1 - zl) * 512, 512), 512)
    mine = pl.ds(pl.multiple_of(zl * 512, 512), 512)

    def total(r, cols):
        return own[r, cols] + rec2[0, r, cols].astype(F32) + rec2[1, r, cols].astype(F32)

    def give(i, _):
        r = pl.ds(pl.multiple_of(i * 16, 16), 16)
        zsend[r] = total(r, theirs).astype(BF16)
        return 0

    lax.fori_loop(0, 32, give, 0)
    copies[6].start()
    copies[6].wait_recv()

    def last(i, _):
        r = pl.ds(pl.multiple_of(i * 16, 16), 16)
        lg_ref[r] = (total(r, mine) + zrec[r].astype(F32)).astype(BF16)
        return 0

    lax.fori_loop(0, 32, last, 0)
    gather.finish()
    for n in range(7):
        copies[n].wait_send()


def density(trial, xloc, colloc):
    rows = trial.shape[0]
    hbm = pl.BlockSpec(memory_space=pl.ANY)
    vmem = pl.BlockSpec(memory_space=pltpu.VMEM)
    return pl.pallas_call(
        density_kernel,
        out_shape=(
            jax.ShapeDtypeStruct((ROWS, 512), BF16),
            jax.ShapeDtypeStruct((2, 4) + colloc.shape, BF16),
        ),
        in_specs=[hbm, vmem, hbm],
        out_specs=(vmem, hbm),
        scratch_shapes=[
            pltpu.VMEM((16, rows, 2, NOCC), BF16),
            pltpu.VMEM((rows, 256), BF16),
            pltpu.VMEM((ROWS, 1024), BF16),
            pltpu.VMEM((2, ROWS, 1024), BF16),
            pltpu.VMEM((ROWS, 1024), F32),
            pltpu.VMEM((2, 256, 1024), BF16),
            pltpu.VMEM((2, ROWS, 1024), BF16),
            pltpu.VMEM((ROWS, 512), BF16),
            pltpu.VMEM((ROWS, 512), BF16),
            pltpu.SemaphoreType.DMA((16,)),
            pltpu.SemaphoreType.DMA((7,)),
            pltpu.SemaphoreType.DMA((7,)),
            pltpu.SemaphoreType.DMA((8,)),
            pltpu.SemaphoreType.DMA((8,)),
            pltpu.SemaphoreType.DMA,
        ],
        compiler_params=pltpu.CompilerParams(
            vmem_limit_bytes=56 << 20, collective_id=0, has_side_effects=True
        ),
        cost_estimate=pl.CostEstimate(
            flops=7 * 10**9, bytes_accessed=150 * 10**6, transcendentals=0
        ),
        name="density",
    )(trial, xloc, colloc)


def pair_kernel(lg_ref, og_ref, kern_ref, eall_ref, e, send, recv, local):
    gather = GatherY(e, eall_ref, send, recv, local)
    for b in range(4):
        r = pl.ds(b * BLK, BLK)
        ore = og_ref[r, :NOCC]
        oim = og_ref[r, NOCC:]
        w = jnp.concatenate(
            [
                jnp.concatenate([ore, oim], axis=1),
                jnp.concatenate([-oim, ore], axis=1),
            ],
            axis=0,
        ).astype(BF16)
        kern = kern_ref[b]
        both = jnp.concatenate([kern, kern], axis=1)
        for v in range(2):
            cols = pl.ds(v * 256, 256)
            rho = lax.dot_general(
                lg_ref[r, cols], w, (((1,), (1,)), ((), ())), preferred_element_type=F32
            )
            m = (rho * both).astype(BF16)
            e[b, :, cols] = jnp.dot(m, w, preferred_element_type=F32).astype(BF16)
    greet([gather.right, gather.left, gather.twin])
    gather.start()
    gather.forward()
    gather.finish()


def pair(lg, og, kern):
    vmem = pl.BlockSpec(memory_space=pltpu.VMEM)
    return pl.pallas_call(
        pair_kernel,
        out_shape=jax.ShapeDtypeStruct((2, 4, 4, BLK, 512), BF16),
        in_specs=[vmem] * 3,
        out_specs=vmem,
        scratch_shapes=[
            pltpu.VMEM((4, BLK, 512), BF16),
            pltpu.SemaphoreType.DMA((8,)),
            pltpu.SemaphoreType.DMA((8,)),
            pltpu.SemaphoreType.DMA,
        ],
        compiler_params=pltpu.CompilerParams(
            vmem_limit_bytes=40 << 20, collective_id=1, has_side_effects=True
        ),
        name="pair",
    )(lg, og, kern)


def panel_kernel(idx_ref, x_ref, e_ref, keep_ref, give_ref, acc):
    def row(r, _):
        acc[...] = jnp.zeros_like(acc)

        def batch(j, _):
            s = idx_ref[r, j]

            @pl.when(s < SIG)
            def _():
                at = pl.multiple_of(s * BLK, BLK)
                acc[...] += lax.dot_general(
                    x_ref[j, :, pl.ds(at, BLK)], e_ref[j], (((0,), (0,)), ((), ())),
                    preferred_element_type=F32,
                )

            return 0

        lax.fori_loop(0, 32, batch, 0)

        @pl.when(r < 6)
        def _():
            keep_ref[jnp.minimum(r, 5)] = acc[...]

        @pl.when(r >= 6)
        def _():
            give_ref[jnp.maximum(r - 6, 0)] = acc[...].astype(BF16)

        return 0

    lax.fori_loop(0, 12, row, 0)


def panel(idx, xall, eall):
    vmem = pl.BlockSpec(memory_space=pltpu.VMEM)
    return pl.pallas_call(
        panel_kernel,
        out_shape=(
            jax.ShapeDtypeStruct((6, BLK, 512), F32),
            jax.ShapeDtypeStruct((6, BLK, 512), BF16),
        ),
        in_specs=[pl.BlockSpec(memory_space=pltpu.SMEM), vmem, vmem],
        out_specs=(vmem, vmem),
        scratch_shapes=[pltpu.VMEM((BLK, 512), F32)],
        compiler_params=pltpu.CompilerParams(vmem_limit_bytes=48 << 20),
        name="panel",
    )(idx, xall, eall)


def place_of(ids, wanted):
    hit = ids[..., None, :] == wanted[..., :, None]
    where = jnp.arange(SIG, dtype=jnp.int32)
    return SIG + jnp.sum(jnp.where(hit, where - SIG, 0), axis=-1).astype(jnp.int32)


def on_device(trial, occupied, colloc, blocks, coords, weights):
    zh, y, c, x, zl = coords_of()
    a = lax.axis_index("ao")
    g = lax.axis_index("grid")
    nloc = trial.shape[0] // BLK
    local = a * nloc + jnp.arange(nloc, dtype=jnp.int32)
    xloc, od = prep(place_of(blocks, local), colloc, occupied)
    og = lax.psum(od, "ao")

    table = lax.all_gather(blocks, "grid").reshape(2, 4, 2, 4, SIG)
    lg, xall = density(trial, xloc, colloc)

    differ = coords[:, :, :, None] - coords[:, :, None, :]
    square = jnp.sum(differ * differ, axis=1)
    kern = weights[:, :, None] * weights[:, None, :] / jnp.sqrt(square + 0.25)
    eall = pair(lg, og.astype(BF16), kern)

    half = lax.dynamic_index_in_dim(table, zh, 0, keepdims=False)
    ys = lax.rem(y + jnp.array([0, 3, 1, 2], jnp.int32), 4)
    cs = jnp.stack([c, 1 - c])
    ids = half[ys][:, cs].transpose(1, 0, 2, 3).reshape(32, SIG)
    step = jnp.arange(6, dtype=jnp.int32)
    first = (y * 2 + c) * 6
    rows = jnp.concatenate([zh * 48 + first + step, (1 - zh) * 48 + first + step])
    idx = place_of(ids, rows).T
    keep, give = panel(
        idx, xall.reshape(32, BLK, SIG * BLK), eall.reshape(32, BLK, 512)
    )
    n = lax.axis_size("grid")
    got = lax.ppermute(give, "grid", [(i, (i + n // 2) % n) for i in range(n)])
    total = keep + got.astype(F32)
    return total.reshape(6 * BLK, 2, 2, NOCC).transpose(1, 0, 2, 3)


def solution(mesh):
    in_specs = (
        P("ao", None, None, None),
        P("ao", None, None),
        P("grid", None, None),
        P("grid", None),
        P("grid", None, None),
        P("grid", None),
    )
    out_specs = P("ao", "grid", None, None)
    return jax.shard_map(
        on_device, mesh=mesh, in_specs=in_specs, out_specs=out_specs, check_vma=False
    )
```

```python
import functools
import jax
import jax.numpy as jnp
from jax import lax
from jax.experimental import pallas as pl
from jax.experimental.pallas import tpu as pltpu
from jax.sharding import PartitionSpec as P

BLK = 128
NOCC = 128
SIG = 12
F32 = jnp.float32
BF16 = jnp.bfloat16
MESH = pl.DeviceIdType.MESH
ROWS = 512


def coords_of():
    g = lax.axis_index("grid")
    a = lax.axis_index("ao")
    return g // 8, lax.rem(g // 2, 4), lax.rem(g, 2), a // 2, lax.rem(a, 2)


def device_at(zh, y, c, x, zl):
    return (zh * 8 + y * 2 + c, x * 2 + zl)


class GatherY:
    def __init__(self, own, slots, first, count, base, send, recv):
        self.own, self.slots, self.base = own, slots, base
        self.send, self.recv = send, recv
        half = count // 2
        self.every = pl.ds(first, count)
        self.lo, self.hi = pl.ds(first, half), pl.ds(first + half, half)
        zh, y, c, x, zl = coords_of()
        self.right = device_at(zh, lax.rem(y + 1, 4), c, x, zl)
        self.left = device_at(zh, lax.rem(y + 3, 4), c, x, zl)
        self.twin = device_at(zh, y, 1 - c, x, zl)

    def at(self, n):
        s, own, lo, hi, every = self.slots, self.own, self.lo, self.hi, self.every
        src, dst, to = [
            (own.at[lo], s.at[0, 1, lo], self.right),
            (own.at[hi], s.at[0, 2, hi], self.left),
            (own.at[hi], s.at[0, 1, hi], self.right),
            (own.at[lo], s.at[0, 2, lo], self.left),
            (own.at[every], s.at[1, 0, every], self.twin),
            (s.at[0, 1, lo], s.at[0, 3, lo], self.right),
            (s.at[0, 2, hi], s.at[0, 3, hi], self.left),
            (s.at[0, 1, every], s.at[1, 1, every], self.twin),
            (s.at[0, 2, every], s.at[1, 2, every], self.twin),
            (s.at[0, 3, every], s.at[1, 3, every], self.twin),
        ][n]
        return remote(self.send, self.recv, self.base + n, src, dst, to)

    def start_first(self):
        for n in (0, 1):
            self.at(n).start()

    def start_second(self):
        for n in (2, 3, 4):
            self.at(n).start()

    def forward(self):
        for n in (0, 1):
            self.at(n).wait_recv()
            self.at(n + 5).start()

    def spread(self):
        for n in (2, 3):
            self.at(n).wait_recv()
            self.at(n + 5).start()

    def spread_opposite(self):
        for n in (5, 6):
            self.at(n).wait_recv()
        self.at(9).start()

    def finish(self):
        for n in (4, 7, 8, 9):
            self.at(n).wait_recv()
        for n in range(10):
            self.at(n).wait_send()


def remote(send, recv, n, src, dst, to):
    return pltpu.make_async_remote_copy(
        src_ref=src, dst_ref=dst, send_sem=send.at[n], recv_sem=recv.at[n],
        device_id=to, device_id_type=MESH,
    )


def greet(peers):
    barrier = pltpu.get_barrier_semaphore()
    for peer in peers:
        pl.semaphore_signal(barrier, inc=1, device_id=peer, device_id_type=MESH)
    pl.semaphore_wait(barrier, len(peers))


def rows_of(start, size):
    return pl.ds(pl.multiple_of(start, size), size)


def main_kernel(
    idx_ref, trial_ref, x_ref, occ_ref, ids_ref, kern_ref,
    xall_ref, eall_ref, idall_ref,
    buf, w, xpad, xloc, opp, part, own, rec1, rec2, zsend, zrec, lg, od, orec, og,
    load_sem, send, recv, osend, orecv, gsend, grecv, local,
):
    zh, y, c, x, zl = coords_of()
    a = x * 2 + zl
    right = device_at(zh, y, c, lax.rem(x + 1, 4), zl)
    left = device_at(zh, y, c, lax.rem(x + 3, 4), zl)
    across = device_at(zh, y, c, x, 1 - zl)
    order = [lax.rem(x + d, 4) for d in (2, 1, 3, 0)]

    def load(v):
        return pltpu.make_async_copy(trial_ref.at[:, v], buf.at[v], load_sem.at[v])

    for dest in order:
        for t in range(4):
            load(dest * 4 + t).start()

    ao_peers = [(lax.axis_index("grid"), lax.rem(a + d, 8)) for d in range(1, 8)]
    grid_peers = [
        (device_at(zh, lax.rem(y + d, 4), c if same else 1 - c, x, zl), 0 if same else 1, slot)
        for d, slot in ((0, 0), (1, 1), (3, 2), (2, 3))
        for same in (True, False)
        if d or not same
    ]
    greet(ao_peers + [peer for peer, _, _ in grid_peers])

    gx = GatherY(x_ref, xall_ref, 0, 4, 0, gsend, grecv)
    ge = [GatherY(eall_ref.at[0, 0], eall_ref, 2 * p, 2, 10 + 10 * p, gsend, grecv) for p in (0, 1)]
    gx.start_first()
    keep = pltpu.make_async_copy(x_ref, xall_ref.at[0, 0], local)
    keep.start()
    ids = [
        remote(gsend, grecv, 30 + n, ids_ref, idall_ref.at[i, slot], peer)
        for n, (peer, i, slot) in enumerate(grid_peers)
    ]
    for copy in ids:
        copy.start()
    idall_ref[0, 0] = ids_ref[...]

    for b in range(4):
        for s in range(SIG):
            xpad[b, s] = x_ref[b, :, s * BLK : (s + 1) * BLK]
        xpad[b, SIG] = jnp.zeros((BLK, BLK), BF16)
    for b in range(4):
        for l in range(xloc.shape[1] // BLK):
            xloc[b * BLK : (b + 1) * BLK, l * BLK : (l + 1) * BLK] = xpad[b, idx_ref[b, l]]

    def split(src):
        def some(k, _):
            k = pl.ds(pl.multiple_of(k * 256, 256), 256)
            both = src[k].astype(F32)
            w[k, :NOCC] = both[:, 0, :].astype(BF16)
            w[k, NOCC:] = both[:, 1, :].astype(BF16)
            return 0

        lax.fori_loop(0, w.shape[0] // 256, some, 0)

    split(occ_ref)
    od[...] = jnp.dot(xloc[...], w[...], preferred_element_type=F32)
    osum = [
        remote(osend, orecv, d - 1, od.at[rows_of(lax.rem(a + d, 8) * 64, 64)], orec.at[d - 1], ao_peers[d - 1])
        for d in range(1, 8)
    ]
    for copy in osum:
        copy.start()

    def densities(dest, store):
        def one(t, _):
            v = dest * 4 + t
            load(v).wait()
            split(buf.at[v])
            store(
                pl.ds(pl.multiple_of(t * 256, 256), 256),
                jnp.dot(xloc[...], w[...], preferred_element_type=F32),
            )
            return 0

        lax.fori_loop(0, 4, one, 0)

    batch = [pl.ds(b * BLK, BLK) for b in range(4)]
    to_opp = [remote(send, recv, b, opp.at[batch[b]], rec1.at[batch[b]], (right, left)[b % 2]) for b in range(4)]
    to_right = [remote(send, recv, 4 + b, part.at[0, batch[b]], rec2.at[0, batch[b]], right) for b in range(4)]
    to_left = [remote(send, recv, 8 + b, part.at[1, batch[b]], rec2.at[1, batch[b]], left) for b in range(4)]
    half = [pl.ds(256 * p, 256) for p in (0, 1)]
    to_pair = [remote(send, recv, 12 + p, zsend.at[half[p]], zrec.at[half[p]], across) for p in (0, 1)]

    def store_opp(cols, value):
        opp[:, cols] = value.astype(BF16)

    def store_side(side):
        def store(cols, value):
            for b in range(4):
                piece = value[b * BLK : (b + 1) * BLK]
                if b % 2 == side:
                    own[batch[b], cols] = piece
                else:
                    part[side, batch[b], cols] = piece.astype(BF16)

        return store

    def store_own(cols, value):
        own[:, cols] = value

    def add(side, b):
        to_opp[b].wait_recv()

        def some(i, _):
            r = rows_of(b * BLK + i * 16, 16)
            part[side, r] = (own[r] + rec1[r].astype(F32)).astype(BF16)
            return 0

        lax.fori_loop(0, BLK // 16, some, 0)

    densities(order[0], store_opp)
    for copy in to_opp:
        copy.start()
    gx.start_second()
    for copy in osum:
        copy.wait_recv()
    mine64 = rows_of(a * 64, 64)
    og[mine64] = (od[mine64] + sum(orec[n] for n in range(7))).astype(BF16)
    ogat = [
        remote(osend, orecv, 7 + d - 1, og.at[mine64], og.at[mine64], ao_peers[d - 1])
        for d in range(1, 8)
    ]
    for copy in ogat:
        copy.start()

    densities(order[1], store_side(0))
    to_right[1].start()
    add(0, 0)
    to_right[0].start()
    to_right[3].start()
    add(0, 2)
    to_right[2].start()
    gx.forward()
    densities(order[2], store_side(1))
    to_left[0].start()
    add(1, 1)
    to_left[1].start()
    to_left[2].start()
    add(1, 3)
    to_left[3].start()
    densities(order[3], store_own)
    gx.spread()

    theirs = pl.ds(pl.multiple_of((1 - zl) * 512, 512), 512)
    mine = pl.ds(pl.multiple_of(zl * 512, 512), 512)

    def total(r, cols):
        return own[r, cols] + rec2[0, r, cols].astype(F32) + rec2[1, r, cols].astype(F32)

    for p in (0, 1):
        for b in (2 * p, 2 * p + 1):
            to_right[b].wait_recv()
            to_left[b].wait_recv()

        def give(i, _):
            r = rows_of(256 * p + i * 16, 16)
            zsend[r] = total(r, theirs).astype(BF16)
            return 0

        lax.fori_loop(0, 16, give, 0)
        to_pair[p].start()
    for copy in ogat:
        copy.wait_recv()
    gx.spread_opposite()

    for p in (0, 1):
        to_pair[p].wait_recv()

        def last(i, _):
            r = rows_of(256 * p + i * 16, 16)
            lg[r] = (total(r, mine) + zrec[r].astype(F32)).astype(BF16)
            return 0

        lax.fori_loop(0, 16, last, 0)
        for b in (2 * p, 2 * p + 1):
            ore = og[batch[b], :NOCC].astype(F32)
            oim = og[batch[b], NOCC:].astype(F32)
            ww = jnp.concatenate(
                [
                    jnp.concatenate([ore, oim], axis=1),
                    jnp.concatenate([-oim, ore], axis=1),
                ],
                axis=0,
            ).astype(BF16)
            both = jnp.concatenate([kern_ref[b], kern_ref[b]], axis=1)
            for v in range(2):
                cols = pl.ds(v * 256, 256)
                rho = lax.dot_general(
                    lg[batch[b], cols], ww, (((1,), (1,)), ((), ())), preferred_element_type=F32
                )
                m = (rho * both).astype(BF16)
                eall_ref[0, 0, b, :, cols] = jnp.dot(m, ww, preferred_element_type=F32).astype(BF16)
        ge[p].start_first()
        ge[p].start_second()

    for p in (0, 1):
        ge[p].forward()
        ge[p].spread()
    for p in (0, 1):
        ge[p].spread_opposite()
    for gather in [gx] + ge:
        gather.finish()
    keep.wait()
    for copy in ids:
        copy.wait()
    for copy in ogat + osum + to_opp + to_right + to_left + to_pair:
        copy.wait_send()


def exchange_step(idx, trial, colloc, occupied, ids, kern):
    rows = trial.shape[0]
    hbm = pl.BlockSpec(memory_space=pl.ANY)
    vmem = pl.BlockSpec(memory_space=pltpu.VMEM)
    return pl.pallas_call(
        main_kernel,
        out_shape=(
            jax.ShapeDtypeStruct((2, 4) + colloc.shape, BF16),
            jax.ShapeDtypeStruct((2, 4, 4, BLK, 512), BF16),
            jax.ShapeDtypeStruct((2, 4) + ids.shape, jnp.int32),
        ),
        in_specs=[pl.BlockSpec(memory_space=pltpu.SMEM), hbm, vmem, vmem, vmem, vmem],
        out_specs=(hbm, vmem, vmem),
        scratch_shapes=[
            pltpu.VMEM((16, rows, 2, NOCC), BF16),
            pltpu.VMEM((rows, 256), BF16),
            pltpu.VMEM((4, SIG + 1, BLK, BLK), BF16),
            pltpu.VMEM((ROWS, rows), BF16),
            pltpu.VMEM((ROWS, 1024), BF16),
            pltpu.VMEM((2, ROWS, 1024), BF16),
            pltpu.VMEM((ROWS, 1024), F32),
            pltpu.VMEM((ROWS, 1024), BF16),
            pltpu.VMEM((2, ROWS, 1024), BF16),
            pltpu.VMEM((ROWS, 512), BF16),
            pltpu.VMEM((ROWS, 512), BF16),
            pltpu.VMEM((ROWS, 512), BF16),
            pltpu.VMEM((ROWS, 2 * NOCC), F32),
            pltpu.VMEM((7, ROWS // 8, 2 * NOCC), F32),
            pltpu.VMEM((ROWS, 2 * NOCC), BF16),
            pltpu.SemaphoreType.DMA((16,)),
            pltpu.SemaphoreType.DMA((14,)),
            pltpu.SemaphoreType.DMA((14,)),
            pltpu.SemaphoreType.DMA((14,)),
            pltpu.SemaphoreType.DMA((14,)),
            pltpu.SemaphoreType.DMA((37,)),
            pltpu.SemaphoreType.DMA((37,)),
            pltpu.SemaphoreType.DMA,
        ],
        compiler_params=pltpu.CompilerParams(
            vmem_limit_bytes=58 << 20, collective_id=0, has_side_effects=True
        ),
        name="exchange_step",
    )(idx, trial, colloc, occupied, ids, kern)


def panel_kernel(ids_ref, base_ref, x_ref, e_ref, out_ref, acc):
    acc[...] = jnp.zeros_like(acc)
    base = base_ref[0]

    def batch(j, _):
        for s in range(SIG):
            r = ids_ref[j, s] - base

            @pl.when((r >= 0) & (r < 6))
            def _():
                acc[jnp.clip(r, 0, 5)] += lax.dot_general(
                    x_ref[j, :, s * BLK : (s + 1) * BLK], e_ref[j], (((0,), (0,)), ((), ())),
                    preferred_element_type=F32,
                )

        return 0

    lax.fori_loop(0, 32, batch, 0)
    out_ref[...] = acc[...].astype(out_ref.dtype)


def panel(ids, base, xall, eall, dtype):
    vmem = pl.BlockSpec(memory_space=pltpu.VMEM)
    smem = pl.BlockSpec(memory_space=pltpu.SMEM)
    return pl.pallas_call(
        panel_kernel,
        out_shape=jax.ShapeDtypeStruct((6, BLK, 512), dtype),
        in_specs=[smem, smem, vmem, vmem],
        out_specs=vmem,
        scratch_shapes=[pltpu.VMEM((6, BLK, 512), F32)],
        compiler_params=pltpu.CompilerParams(vmem_limit_bytes=48 << 20),
        cost_estimate=pl.CostEstimate(flops=10**9, bytes_accessed=20 * 10**6, transcendentals=0),
        name="panel",
    )(ids, base, xall, eall)


def place_of(ids, wanted):
    hit = ids[..., None, :] == wanted[..., :, None]
    where = jnp.arange(SIG, dtype=jnp.int32)
    return SIG + jnp.sum(jnp.where(hit, where - SIG, 0), axis=-1).astype(jnp.int32)


def on_device(trial, occupied, colloc, blocks, coords, weights):
    zh, y, c, x, zl = coords_of()
    nloc = trial.shape[0] // BLK
    local = lax.axis_index("ao") * nloc + jnp.arange(nloc, dtype=jnp.int32)
    differ = coords[:, :, :, None] - coords[:, :, None, :]
    square = jnp.sum(differ * differ, axis=1)
    kern = weights[:, :, None] * weights[:, None, :] / jnp.sqrt(square + 0.25)
    padded = jnp.pad(blocks, ((0, 4), (0, BLK - SIG)))
    xall, eall, idall = exchange_step(
        place_of(blocks, local), trial, colloc, occupied, padded, kern
    )
    ids = idall[:, :, :4, :SIG].reshape(32, SIG)
    xs = xall.reshape(32, BLK, SIG * BLK)
    es = eall.reshape(32, BLK, 512)
    first = (y * 2 + c) * 6
    give = panel(ids, ((1 - zh) * 48 + first)[None].astype(jnp.int32), xs, es, BF16)
    n = lax.axis_size("grid")
    got = lax.ppermute(give, "grid", [(i, (i + n // 2) % n) for i in range(n)])
    keep = panel(ids, (zh * 48 + first)[None].astype(jnp.int32), xs, es, F32)
    total = keep + got.astype(F32)
    return total.reshape(6 * BLK, 2, 2, NOCC).transpose(1, 0, 2, 3)


def solution(mesh):
    in_specs = (
        P("ao", None, None, None),
        P("ao", None, None),
        P("grid", None, None),
        P("grid", None),
        P("grid", None, None),
        P("grid", None),
    )
    out_specs = P("ao", "grid", None, None)
    return jax.shard_map(
        on_device, mesh=mesh, in_specs=in_specs, out_specs=out_specs, check_vma=False
    )
```

```python
import functools
import jax
import jax.numpy as jnp
from jax import lax
from jax.experimental import pallas as pl
from jax.experimental.pallas import tpu as pltpu
from jax.sharding import PartitionSpec as P

BLK = 128
NOCC = 128
SIG = 12
F32 = jnp.float32
BF16 = jnp.bfloat16
MESH = pl.DeviceIdType.MESH
ROWS = 512


def coords_of():
    g = lax.axis_index("grid")
    a = lax.axis_index("ao")
    return g // 8, lax.rem(g // 2, 4), lax.rem(g, 2), a // 2, lax.rem(a, 2)


def device_at(zh, y, c, x, zl):
    return (zh * 8 + y * 2 + c, x * 2 + zl)


class GatherY:
    def __init__(self, own, slots, first, count, base, send, recv, tail=()):
        self.own, self.slots, self.base = own, slots, base
        self.send, self.recv, self.tail = send, recv, tail
        half = count // 2
        self.every = pl.ds(first, count)
        self.lo, self.hi = pl.ds(first, half), pl.ds(first + half, half)
        zh, y, c, x, zl = coords_of()
        self.right = device_at(zh, lax.rem(y + 1, 4), c, x, zl)
        self.left = device_at(zh, lax.rem(y + 3, 4), c, x, zl)
        self.twin = device_at(zh, y, 1 - c, x, zl)

    def at(self, n):
        own, slots, lo, hi, every = self.own, self.slots, self.lo, self.hi, self.every

        def o(b):
            return own.at[(b,) + self.tail]

        def s(i, slot, b):
            return slots(i, slot).at[(b,) + self.tail]

        src, dst, to = [
            (o(lo), s(0, 1, lo), self.right),
            (o(hi), s(0, 2, hi), self.left),
            (o(hi), s(0, 1, hi), self.right),
            (o(lo), s(0, 2, lo), self.left),
            (o(every), s(1, 0, every), self.twin),
            (s(0, 1, lo), s(0, 3, lo), self.right),
            (s(0, 2, hi), s(0, 3, hi), self.left),
            (s(0, 1, every), s(1, 1, every), self.twin),
            (s(0, 2, every), s(1, 2, every), self.twin),
            (s(0, 3, every), s(1, 3, every), self.twin),
        ][n]
        return remote(self.send, self.recv, self.base + n, src, dst, to)

    def start_first(self):
        for n in (0, 1):
            self.at(n).start()

    def start_second(self):
        for n in (2, 3, 4):
            self.at(n).start()

    def forward(self):
        for n in (0, 1):
            self.at(n).wait_recv()
            self.at(n + 5).start()

    def spread(self):
        for n in (2, 3):
            self.at(n).wait_recv()
            self.at(n + 5).start()

    def spread_opposite(self):
        for n in (5, 6):
            self.at(n).wait_recv()
        self.at(9).start()

    def arrived(self, *which):
        for n in which:
            self.at(n).wait_recv()

    def sent(self):
        for n in range(10):
            self.at(n).wait_send()


def remote(send, recv, n, src, dst, to):
    return pltpu.make_async_remote_copy(
        src_ref=src, dst_ref=dst, send_sem=send.at[n], recv_sem=recv.at[n],
        device_id=to, device_id_type=MESH,
    )


def greet(peers):
    barrier = pltpu.get_barrier_semaphore()
    for peer in peers:
        pl.semaphore_signal(barrier, inc=1, device_id=peer, device_id_type=MESH)
    pl.semaphore_wait(barrier, len(peers))


def rows_of(start, size):
    return pl.ds(pl.multiple_of(start, size), size)


def main_kernel(
    inv_ref, trial_ref, x_ref, occ_ref, place_ref, coords_ref, weights_ref, out_ref,
    x00, x01, x02, x03, x10, x11, x12, x13, eall, places, table, kern, acc, give, got,
    buf, w, xloc, opp, part, own, rec1, rec2, zsend, zrec, lg, od, orec, og,
    load_sem, send, recv, osend, orecv, gsend, grecv, hsend, hrecv, local,
):
    zh, y, c, x, zl = coords_of()
    a = x * 2 + zl
    beyond = device_at(1 - zh, y, c, x, zl)
    right = device_at(zh, y, c, lax.rem(x + 1, 4), zl)
    left = device_at(zh, y, c, lax.rem(x + 3, 4), zl)
    across = device_at(zh, y, c, x, 1 - zl)
    order = [lax.rem(x + d, 4) for d in (2, 1, 3, 0)]

    def load(v):
        return pltpu.make_async_copy(trial_ref.at[:, v], buf.at[v], load_sem.at[v])

    for dest in order:
        for t in range(4):
            load(dest * 4 + t).start()

    ao_peers = [(lax.axis_index("grid"), lax.rem(a + d, 8)) for d in range(1, 8)]
    grid_peers = [
        (device_at(zh, lax.rem(y + d, 4), c if same else 1 - c, x, zl), 0 if same else 1, slot)
        for d, slot in ((0, 0), (1, 1), (3, 2), (2, 3))
        for same in (True, False)
        if d or not same
    ]
    greet(ao_peers + [peer for peer, _, _ in grid_peers] + [beyond])

    for b in range(4):
        for n in range(SIG):
            x00[b, n] = x_ref[b, :, n * BLK : (n + 1) * BLK]
    xs = [[x00, x01, x02, x03], [x10, x11, x12, x13]]
    gx = GatherY(x00, lambda i, slot: xs[i][slot], 0, 4, 0, gsend, grecv, (pl.ds(0, SIG),))
    ge = [
        GatherY(eall.at[0, 0], lambda i, slot: eall.at[i, slot], 2 * p, 2, 10 + 10 * p, gsend, grecv)
        for p in (0, 1)
    ]
    gx.start_first()
    tables = [
        remote(gsend, grecv, 30 + n, place_ref, places.at[i, slot], peer)
        for n, (peer, i, slot) in enumerate(grid_peers)
    ]
    for copy in tables:
        copy.start()
    places[0, 0] = place_ref[...]
    for i in range(2):
        for slot in range(4):
            for b in range(4):
                xs[i][slot][b, SIG] = jnp.zeros((BLK, BLK), BF16)
    for b in range(4):
        for l in range(xloc.shape[1] // BLK):
            xloc[b * BLK : (b + 1) * BLK, l * BLK : (l + 1) * BLK] = x00[
                b, inv_ref[b, a * (xloc.shape[1] // BLK) + l]
            ]

    def split(src):
        def some(k, _):
            k = pl.ds(pl.multiple_of(k * 256, 256), 256)
            both = src[k].astype(F32)
            w[k, :NOCC] = both[:, 0, :].astype(BF16)
            w[k, NOCC:] = both[:, 1, :].astype(BF16)
            return 0

        lax.fori_loop(0, w.shape[0] // 256, some, 0)

    split(occ_ref)
    od[...] = jnp.dot(xloc[...], w[...], preferred_element_type=F32)
    osum = [
        remote(osend, orecv, d - 1, od.at[rows_of(lax.rem(a + d, 8) * 64, 64)], orec.at[d - 1], ao_peers[d - 1])
        for d in range(1, 8)
    ]
    for copy in osum:
        copy.start()

    def densities(dest, store):
        def one(t, _):
            v = dest * 4 + t
            load(v).wait()
            split(buf.at[v])
            store(
                pl.ds(pl.multiple_of(t * 256, 256), 256),
                jnp.dot(xloc[...], w[...], preferred_element_type=F32),
            )
            return 0

        lax.fori_loop(0, 4, one, 0)

    batch = [pl.ds(b * BLK, BLK) for b in range(4)]
    to_opp = [remote(send, recv, b, opp.at[batch[b]], rec1.at[batch[b]], (right, left)[b % 2]) for b in range(4)]
    to_right = [remote(send, recv, 4 + b, part.at[0, batch[b]], rec2.at[0, batch[b]], right) for b in range(4)]
    to_left = [remote(send, recv, 8 + b, part.at[1, batch[b]], rec2.at[1, batch[b]], left) for b in range(4)]
    half = [pl.ds(256 * p, 256) for p in (0, 1)]
    to_pair = [remote(send, recv, 12 + p, zsend.at[half[p]], zrec.at[half[p]], across) for p in (0, 1)]

    def store_opp(cols, value):
        opp[:, cols] = value.astype(BF16)

    def store_side(side):
        def store(cols, value):
            for b in range(4):
                piece = value[b * BLK : (b + 1) * BLK]
                if b % 2 == side:
                    own[batch[b], cols] = piece
                else:
                    part[side, batch[b], cols] = piece.astype(BF16)

        return store

    def store_own(cols, value):
        own[:, cols] = value

    def add(side, b):
        to_opp[b].wait_recv()

        def some(i, _):
            r = rows_of(b * BLK + i * 16, 16)
            part[side, r] = (own[r] + rec1[r].astype(F32)).astype(BF16)
            return 0

        lax.fori_loop(0, BLK // 16, some, 0)

    densities(order[0], store_opp)
    for copy in to_opp:
        copy.start()
    gx.start_second()
    for copy in osum:
        copy.wait_recv()
    mine64 = rows_of(a * 64, 64)
    og[mine64] = (od[mine64] + sum(orec[n] for n in range(7))).astype(BF16)
    ogat = [
        remote(osend, orecv, 7 + d - 1, og.at[mine64], og.at[mine64], ao_peers[d - 1])
        for d in range(1, 8)
    ]
    for copy in ogat:
        copy.start()

    densities(order[1], store_side(0))
    to_right[1].start()
    add(0, 0)
    to_right[0].start()
    to_right[3].start()
    add(0, 2)
    to_right[2].start()
    gx.forward()
    densities(order[2], store_side(1))
    to_left[0].start()
    add(1, 1)
    to_left[1].start()
    to_left[2].start()
    add(1, 3)
    to_left[3].start()
    densities(order[3], store_own)
    gx.spread()

    def spread_row(row):
        return jnp.broadcast_to(row, (BLK, BLK))

    for b in range(4):
        square = None
        for k in range(3):
            along = spread_row(coords_ref[k, b : b + 1, :])
            differ = along.T - along
            square = differ * differ if square is None else square + differ * differ
        quad = spread_row(weights_ref[b : b + 1, :])
        kern[b] = quad.T * quad / jnp.sqrt(square + 0.25)
    for copy in tables:
        copy.wait_recv()
    fill = pltpu.make_async_copy(places, table, local)
    fill.start()
    fill.wait()
    acc[...] = jnp.zeros_like(acc)

    theirs = pl.ds(pl.multiple_of((1 - zl) * 512, 512), 512)
    mine = pl.ds(pl.multiple_of(zl * 512, 512), 512)

    def total(r, cols):
        return own[r, cols] + rec2[0, r, cols].astype(F32) + rec2[1, r, cols].astype(F32)

    for p in (0, 1):
        for b in (2 * p, 2 * p + 1):
            to_right[b].wait_recv()
            to_left[b].wait_recv()

        def hand(i, _):
            r = rows_of(256 * p + i * 16, 16)
            zsend[r] = total(r, theirs).astype(BF16)
            return 0

        lax.fori_loop(0, 16, hand, 0)
        to_pair[p].start()
    for copy in ogat:
        copy.wait_recv()
    gx.spread_opposite()

    for p in (0, 1):
        to_pair[p].wait_recv()

        def last(i, _):
            r = rows_of(256 * p + i * 16, 16)
            lg[r] = (total(r, mine) + zrec[r].astype(F32)).astype(BF16)
            return 0

        lax.fori_loop(0, 16, last, 0)
        for b in (2 * p, 2 * p + 1):
            ore = og[batch[b], :NOCC].astype(F32)
            oim = og[batch[b], NOCC:].astype(F32)
            ww = jnp.concatenate(
                [
                    jnp.concatenate([ore, oim], axis=1),
                    jnp.concatenate([-oim, ore], axis=1),
                ],
                axis=0,
            ).astype(BF16)
            both = jnp.concatenate([kern[b], kern[b]], axis=1)
            for v in range(2):
                cols = pl.ds(v * 256, 256)
                rho = lax.dot_general(
                    lg[batch[b], cols], ww, (((1,), (1,)), ((), ())), preferred_element_type=F32
                )
                m = (rho * both).astype(BF16)
                eall[0, 0, b, :, cols] = jnp.dot(m, ww, preferred_element_type=F32).astype(BF16)
        ge[p].start_first()
        ge[p].start_second()

    first = (y * 2 + c) * 6

    def panel(i, slot, start, stop):
        def row(r, _):
            block = jnp.where(r < 6, (1 - zh) * 48 + first + r, zh * 48 + first + r - 6)
            tiles = [xs[i][slot][b, table[i, slot, b, block]] for b in range(4)]
            acc[r] += lax.dot_general(
                jnp.concatenate(tiles, axis=0), eall[i, slot].reshape(4 * BLK, 512),
                (((0,), (0,)), ((), ())), preferred_element_type=F32,
            )
            return 0

        lax.fori_loop(start, stop, row, 0)

    ge[0].forward()
    ge[0].spread()
    panel(0, 0, 0, 12)
    ge[1].forward()
    ge[1].spread()
    for gather in [gx] + ge:
        gather.arrived(4)
    panel(1, 0, 0, 12)
    panel(0, 1, 0, 12)
    panel(0, 2, 0, 12)
    ge[0].spread_opposite()
    ge[1].spread_opposite()
    for gather in [gx] + ge:
        gather.arrived(7, 8)
    panel(1, 1, 0, 12)
    panel(1, 2, 0, 12)
    panel(0, 3, 0, 12)
    for gather in [gx] + ge:
        gather.arrived(9)
    over = [remote(hsend, hrecv, n, give.at[n], got.at[n], beyond) for n in range(2)]
    for n in (0, 1):
        panel(1, 3, 3 * n, 3 * n + 3)
        for r in range(3 * n, 3 * n + 3):
            give[n, r - 3 * n] = acc[r].astype(BF16)
        over[n].start()
    panel(1, 3, 6, 12)
    for r in range(6):
        if r % 3 == 0:
            over[r // 3].wait_recv()
        for v in range(2):
            for k in range(2):
                cols = slice(v * 256 + k * 128, v * 256 + k * 128 + 128)
                out_ref[v, r * BLK : (r + 1) * BLK, k, :] = acc[6 + r, :, cols] + got[
                    r // 3, r % 3, :, cols
                ].astype(F32)
    for gather in [gx] + ge:
        gather.sent()
    for copy in tables + over + ogat + osum + to_opp + to_right + to_left + to_pair:
        copy.wait_send()


def exchange_step(inv, trial, colloc, occupied, coords, weights):
    rows = trial.shape[0]
    hbm = pl.BlockSpec(memory_space=pl.ANY)
    vmem = pl.BlockSpec(memory_space=pltpu.VMEM)
    smem = pl.BlockSpec(memory_space=pltpu.SMEM)
    return pl.pallas_call(
        main_kernel,
        out_shape=jax.ShapeDtypeStruct((2, 6 * BLK, 2, NOCC), F32),
        in_specs=[smem, hbm, vmem, vmem, vmem, vmem, vmem],
        out_specs=vmem,
        scratch_shapes=[
            *[pltpu.VMEM((4, SIG + 1, BLK, BLK), BF16)] * 8,
            pltpu.VMEM((2, 4, 4, BLK, 512), BF16),
            pltpu.VMEM((2, 4) + inv.shape, jnp.int32),
            pltpu.SMEM((2, 4) + inv.shape, jnp.int32),
            pltpu.VMEM((4, BLK, BLK), F32),
            pltpu.VMEM((12, BLK, 512), F32),
            pltpu.VMEM((2, 3, BLK, 512), BF16),
            pltpu.VMEM((2, 3, BLK, 512), BF16),
            pltpu.VMEM((16, rows, 2, NOCC), BF16),
            pltpu.VMEM((rows, 256), BF16),
            pltpu.VMEM((ROWS, rows), BF16),
            pltpu.VMEM((ROWS, 1024), BF16),
            pltpu.VMEM((2, ROWS, 1024), BF16),
            pltpu.VMEM((ROWS, 1024), F32),
            pltpu.VMEM((ROWS, 1024), BF16),
            pltpu.VMEM((2, ROWS, 1024), BF16),
            pltpu.VMEM((ROWS, 512), BF16),
            pltpu.VMEM((ROWS, 512), BF16),
            pltpu.VMEM((ROWS, 512), BF16),
            pltpu.VMEM((ROWS, 2 * NOCC), F32),
            pltpu.VMEM((7, ROWS // 8, 2 * NOCC), F32),
            pltpu.VMEM((ROWS, 2 * NOCC), BF16),
            pltpu.SemaphoreType.DMA((16,)),
            pltpu.SemaphoreType.DMA((14,)),
            pltpu.SemaphoreType.DMA((14,)),
            pltpu.SemaphoreType.DMA((14,)),
            pltpu.SemaphoreType.DMA((14,)),
            pltpu.SemaphoreType.DMA((37,)),
            pltpu.SemaphoreType.DMA((37,)),
            pltpu.SemaphoreType.DMA((2,)),
            pltpu.SemaphoreType.DMA((2,)),
            pltpu.SemaphoreType.DMA,
        ],
        compiler_params=pltpu.CompilerParams(
            vmem_limit_bytes=63 << 20, collective_id=0, has_side_effects=True
        ),
        name="exchange_step",
    )(inv, trial, colloc, occupied, inv, coords, weights)


def place_of(ids, wanted):
    hit = ids[..., None, :] == wanted[..., :, None]
    where = jnp.arange(SIG, dtype=jnp.int32)
    return SIG + jnp.sum(jnp.where(hit, where - SIG, 0), axis=-1).astype(jnp.int32)


def on_device(trial, occupied, colloc, blocks, coords, weights):
    nblk = trial.shape[0] // BLK * lax.axis_size("ao")
    inv = place_of(blocks, jnp.arange(nblk, dtype=jnp.int32))
    inv = jnp.pad(inv, ((0, 4), (0, BLK - nblk)))
    return exchange_step(inv, trial, colloc, occupied, coords.transpose(1, 0, 2), weights)


def solution(mesh):
    in_specs = (
        P("ao", None, None, None),
        P("ao", None, None),
        P("grid", None, None),
        P("grid", None),
        P("grid", None, None),
        P("grid", None),
    )
    out_specs = P("ao", "grid", None, None)
    return jax.shard_map(
        on_device, mesh=mesh, in_specs=in_specs, out_specs=out_specs, check_vma=False
    )
```

```python
import functools
import jax
import jax.numpy as jnp
from jax import lax
from jax.experimental import pallas as pl
from jax.experimental.pallas import tpu as pltpu
from jax.sharding import PartitionSpec as P

BLK = 128
NOCC = 128
SIG = 12
F32 = jnp.float32
BF16 = jnp.bfloat16
MESH = pl.DeviceIdType.MESH
ROWS = 512


def coords_of():
    g = lax.axis_index("grid")
    a = lax.axis_index("ao")
    return g // 8, lax.rem(g // 2, 4), lax.rem(g, 2), a // 2, lax.rem(a, 2)


def device_at(zh, y, c, x, zl):
    return (zh * 8 + y * 2 + c, x * 2 + zl)


class GatherY:
    def __init__(self, own, slots, first, count, base, send, recv, tail=()):
        self.own, self.slots, self.base = own, slots, base
        self.send, self.recv, self.tail = send, recv, tail
        half = count // 2
        self.every = pl.ds(first, count)
        self.lo, self.hi = pl.ds(first, half), pl.ds(first + half, half)
        zh, y, c, x, zl = coords_of()
        self.right = device_at(zh, lax.rem(y + 1, 4), c, x, zl)
        self.left = device_at(zh, lax.rem(y + 3, 4), c, x, zl)
        self.twin = device_at(zh, y, 1 - c, x, zl)

    def at(self, n):
        own, slots, lo, hi, every = self.own, self.slots, self.lo, self.hi, self.every

        def o(b):
            return own.at[(b,) + self.tail]

        def s(i, slot, b):
            return slots(i, slot).at[(b,) + self.tail]

        src, dst, to = [
            (o(lo), s(0, 1, lo), self.right),
            (o(hi), s(0, 2, hi), self.left),
            (o(hi), s(0, 1, hi), self.right),
            (o(lo), s(0, 2, lo), self.left),
            (o(every), s(1, 0, every), self.twin),
            (s(0, 1, lo), s(0, 3, lo), self.right),
            (s(0, 2, hi), s(0, 3, hi), self.left),
            (s(0, 1, every), s(1, 1, every), self.twin),
            (s(0, 2, every), s(1, 2, every), self.twin),
            (s(0, 3, every), s(1, 3, every), self.twin),
        ][n]
        return remote(self.send, self.recv, self.base + n, src, dst, to)

    def start_first(self):
        for n in (0, 1):
            self.at(n).start()

    def start_second(self):
        for n in (2, 3, 4):
            self.at(n).start()

    def forward(self):
        for n in (0, 1):
            self.at(n).wait_recv()
            self.at(n + 5).start()

    def spread(self):
        for n in (2, 3):
            self.at(n).wait_recv()
            self.at(n + 5).start()

    def spread_opposite(self):
        for n in (5, 6):
            self.at(n).wait_recv()
        self.at(9).start()

    def arrived(self, *which):
        for n in which:
            self.at(n).wait_recv()

    def sent(self):
        for n in range(10):
            self.at(n).wait_send()


def remote(send, recv, n, src, dst, to):
    return pltpu.make_async_remote_copy(
        src_ref=src, dst_ref=dst, send_sem=send.at[n], recv_sem=recv.at[n],
        device_id=to, device_id_type=MESH,
    )


def greet(peers):
    barrier = pltpu.get_barrier_semaphore()
    for peer in peers:
        pl.semaphore_signal(barrier, inc=1, device_id=peer, device_id_type=MESH)
    pl.semaphore_wait(barrier, len(peers))


def rows_of(start, size):
    return pl.ds(pl.multiple_of(start, size), size)


def main_kernel(
    inv_ref, trial_ref, x_ref, occ_ref, place_ref, coords_ref, weights_ref, out_ref,
    x00, x01, x02, x03, x10, x11, x12, x13, xpad, e0, e1, places, table, kern, acc, give, got,
    buf, w, xloc, opp, part, own, rec1, rec2, zsend, zrec, lg, od, orec, og,
    load_sem, send, recv, osend, orecv, gsend, grecv, hsend, hrecv, local,
):
    zh, y, c, x, zl = coords_of()
    a = x * 2 + zl
    beyond = device_at(1 - zh, y, c, x, zl)
    right = device_at(zh, y, c, lax.rem(x + 1, 4), zl)
    left = device_at(zh, y, c, lax.rem(x + 3, 4), zl)
    across = device_at(zh, y, c, x, 1 - zl)
    order = [lax.rem(x + d, 4) for d in (2, 1, 3, 0)]

    def load(v):
        return pltpu.make_async_copy(trial_ref.at[:, v], buf.at[v], load_sem.at[v])

    for q in (0, 1):
        for dest in order:
            for t in range(2):
                load(dest * 4 + 2 * t + q).start()

    ao_peers = [(lax.axis_index("grid"), lax.rem(a + d, 8)) for d in range(1, 8)]
    grid_peers = [
        (device_at(zh, lax.rem(y + d, 4), c if same else 1 - c, x, zl), 0 if same else 1, slot)
        for d, slot in ((0, 0), (1, 1), (3, 2), (2, 3))
        for same in (True, False)
        if d or not same
    ]
    greet(ao_peers + [peer for peer, _, _ in grid_peers] + [beyond])

    def split(src):
        def some(k, _):
            k = pl.ds(pl.multiple_of(k * 256, 256), 256)
            both = src[k].astype(F32)
            w[k, :NOCC] = both[:, 0, :].astype(BF16)
            w[k, NOCC:] = both[:, 1, :].astype(BF16)
            return 0

        lax.fori_loop(0, w.shape[0] // 256, some, 0)

    zero = jnp.zeros((BLK, BLK), BF16)
    for b in range(4):
        for n in range(SIG):
            xpad[b, n] = x_ref[b, :, n * BLK : (n + 1) * BLK]
        xpad[b, SIG] = zero
    nloc = xloc.shape[1] // BLK
    for b in range(4):
        for l in range(nloc):
            xloc[b * BLK : (b + 1) * BLK, l * BLK : (l + 1) * BLK] = xpad[b, inv_ref[b, a * nloc + l]]

    split(occ_ref)
    od[...] = jnp.dot(xloc[...], w[...], preferred_element_type=F32)
    osum = [
        remote(osend, orecv, d - 1, od.at[rows_of(lax.rem(a + d, 8) * 64, 64)], orec.at[d - 1], ao_peers[d - 1])
        for d in range(1, 8)
    ]
    for copy in osum:
        copy.start()

    for b in range(4):
        for n in range(SIG):
            x00[b, n] = x_ref[b, :, n * BLK : (n + 1) * BLK].T
    xs = [[x00, x01, x02, x03], [x10, x11, x12, x13]]
    es = [e0, e1]
    gx = GatherY(x00, lambda i, slot: xs[i][slot], 0, 4, 0, gsend, grecv, (pl.ds(0, SIG),))
    ge = [
        GatherY(es[q].at[0, 0], lambda i, slot, q=q: es[q].at[i, slot], 0, 4, 10 + 10 * q, gsend, grecv)
        for q in (0, 1)
    ]
    gx.start_first()
    tables = [
        remote(gsend, grecv, 30 + n, place_ref, places.at[i, slot], peer)
        for n, (peer, i, slot) in enumerate(grid_peers)
    ]
    for copy in tables:
        copy.start()
    places[0, 0] = place_ref[...]
    for i in range(2):
        for slot in range(4):
            for b in range(4):
                xs[i][slot][b, SIG] = zero

    def densities(dest, q, store):
        def one(t, _):
            v = dest * 4 + 2 * t + q
            load(v).wait()
            split(buf.at[v])
            store(
                pl.ds(pl.multiple_of(t * 256, 256), 256),
                jnp.dot(xloc[...], w[...], preferred_element_type=F32),
            )
            return 0

        lax.fori_loop(0, 2, one, 0)

    lo, hi = pl.ds(0, 256), pl.ds(256, 256)
    halves = (lo, hi)
    sides = (right, left)
    to_opp = [
        [remote(send, recv, 2 * q + k, opp.at[q, halves[k]], rec1.at[q, halves[k]], sides[k]) for k in (0, 1)]
        for q in (0, 1)
    ]
    to_side = [
        [
            [
                remote(send, recv, 4 + 4 * q + 2 * k + h, part.at[k, q, halves[h]], rec2.at[k, q, halves[h]], sides[k])
                for h in (0, 1)
            ]
            for k in (0, 1)
        ]
        for q in (0, 1)
    ]
    to_pair = [remote(send, recv, 12 + q, zsend.at[q], zrec.at[q], across) for q in (0, 1)]

    def dens_opp(q):
        def store(cols, value):
            opp[q, :, cols] = value.astype(BF16)

        densities(order[0], q, store)
        for copy in to_opp[q]:
            copy.start()

    def dens_side(k, q):
        def store(cols, value):
            own[q, halves[k], cols] = value[256 * k : 256 * k + 256]
            part[k, q, halves[1 - k], cols] = value[256 - 256 * k : 512 - 256 * k].astype(BF16)

        densities(order[1 + k], q, store)
        to_side[q][k][1 - k].start()

    def add_side(k, q):
        to_opp[q][k].wait_recv()

        def some(i, _):
            r = rows_of(256 * k + i * 16, 16)
            part[k, q, r] = (own[q, r] + rec1[q, r].astype(F32)).astype(BF16)
            return 0

        lax.fori_loop(0, 16, some, 0)
        to_side[q][k][k].start()

    def dens_own(q):
        def store(cols, value):
            own[q, :, cols] = value

        densities(order[3], q, store)

    theirs = pl.ds(pl.multiple_of((1 - zl) * 256, 256), 256)
    mine = pl.ds(pl.multiple_of(zl * 256, 256), 256)

    def total(q, r, cols):
        return own[q, r, cols] + rec2[0, q, r, cols].astype(F32) + rec2[1, q, r, cols].astype(F32)

    def to_z(q):
        for k in (0, 1):
            for h in (0, 1):
                to_side[q][k][h].wait_recv()

        def some(i, _):
            r = rows_of(i * 32, 32)
            zsend[q, r] = total(q, r, theirs).astype(BF16)
            return 0

        lax.fori_loop(0, 16, some, 0)
        to_pair[q].start()

    def pair(q):
        to_pair[q].wait_recv()

        def some(i, _):
            r = rows_of(i * 32, 32)
            lg[r] = (total(q, r, mine) + zrec[q, r].astype(F32)).astype(BF16)
            return 0

        lax.fori_loop(0, 16, some, 0)
        for b in range(4):
            rows = pl.ds(b * BLK, BLK)
            ore = og[rows, :NOCC].astype(F32)
            oim = og[rows, NOCC:].astype(F32)
            ww = jnp.concatenate(
                [
                    jnp.concatenate([ore, oim], axis=1),
                    jnp.concatenate([-oim, ore], axis=1),
                ],
                axis=0,
            ).astype(BF16)
            rho = lax.dot_general(
                lg[rows], ww, (((1,), (1,)), ((), ())), preferred_element_type=F32
            )
            m = (rho * jnp.concatenate([kern[b], kern[b]], axis=1)).astype(BF16)
            es[q][0, 0, b] = jnp.dot(m, ww, preferred_element_type=F32).astype(BF16)
        ge[q].start_first()
        ge[q].start_second()

    first = (y * 2 + c) * 6
    GROUP = 3

    def panel(i, slot, q, start, stop, fresh=False):
        def row(n, _):
            lines = []
            for k in range(GROUP):
                r = n * GROUP + k
                block = jnp.where(r < 6, (1 - zh) * 48 + first + r, zh * 48 + first + r - 6)
                lines.append(
                    jnp.concatenate([xs[i][slot][b, table[i, slot, b, block]] for b in range(4)], axis=1)
                )
            value = jnp.dot(
                jnp.concatenate(lines, axis=0), es[q][i, slot].reshape(4 * BLK, 256),
                preferred_element_type=F32,
            ).reshape(GROUP, BLK, 256)
            at = pl.ds(n * GROUP, GROUP)
            acc[q, at] = value if fresh else acc[q, at] + value
            return 0

        lax.fori_loop(start, stop, row, 0)

    over = [
        [remote(hsend, hrecv, 2 * q + n, give.at[q, n], got.at[q, n], beyond) for n in range(2)]
        for q in (0, 1)
    ]

    def middle(q):
        ge[q].spread_opposite()
        ge[q].arrived(4)
        panel(1, 0, q, 0, 4)
        panel(0, 1, q, 0, 4)
        panel(0, 2, q, 0, 4)
        ge[q].arrived(7, 8)
        panel(1, 1, q, 0, 4)
        panel(1, 2, q, 0, 4)
        panel(0, 3, q, 0, 4)

    def last(q):
        ge[q].arrived(9)
        for n in (0, 1):
            panel(1, 3, q, n, n + 1)
            give[q, n] = acc[q, 3 * n : 3 * n + 3].astype(BF16)
            over[q][n].start()
        panel(1, 3, q, 2, 4)

    def finish(q):
        for r in range(6):
            if r % 3 == 0:
                over[q][r // 3].wait_recv()
            for k in range(2):
                cols = slice(k * 128, k * 128 + 128)
                out_ref[q, r * BLK : (r + 1) * BLK, k, :] = acc[q, 6 + r, :, cols] + got[
                    q, r // 3, r % 3, :, cols
                ].astype(F32)

    dens_opp(0)
    gx.start_second()
    dens_side(0, 0)
    for copy in osum:
        copy.wait_recv()
    mine64 = rows_of(a * 64, 64)
    og[mine64] = (od[mine64] + sum(orec[n] for n in range(7))).astype(BF16)
    ogat = [
        remote(osend, orecv, 7 + d - 1, og.at[mine64], og.at[mine64], ao_peers[d - 1])
        for d in range(1, 8)
    ]
    for copy in ogat:
        copy.start()
    add_side(0, 0)
    dens_side(1, 0)
    add_side(1, 0)
    dens_own(0)
    dens_opp(1)
    gx.forward()
    dens_side(0, 1)
    to_z(0)
    dens_side(1, 1)
    add_side(0, 1)
    add_side(1, 1)

    def spread_row(row):
        return jnp.broadcast_to(row, (BLK, BLK))

    for b in range(4):
        square = None
        for k in range(3):
            along = spread_row(coords_ref[k, b : b + 1, :])
            differ = along.T - along
            square = differ * differ if square is None else square + differ * differ
        quad = spread_row(weights_ref[b : b + 1, :])
        kern[b] = quad.T * quad / jnp.sqrt(square + 0.25)
    for copy in tables + ogat:
        copy.wait_recv()
    fill = pltpu.make_async_copy(places, table, local)
    fill.start()
    pair(0)
    fill.wait()
    dens_own(1)
    gx.spread()
    panel(0, 0, 0, 0, 4, fresh=True)
    ge[0].forward()
    ge[0].spread()
    to_z(1)
    gx.spread_opposite()
    gx.arrived(4, 7, 8)
    pair(1)
    middle(0)
    ge[1].forward()
    ge[1].spread()
    gx.arrived(9)
    last(0)
    panel(0, 0, 1, 0, 4, fresh=True)
    middle(1)
    last(1)
    finish(0)
    finish(1)
    for gather in [gx] + ge:
        gather.sent()
    for q in (0, 1):
        for copy in to_opp[q] + to_side[q][0] + to_side[q][1] + over[q] + [to_pair[q]]:
            copy.wait_send()
    for copy in tables + ogat + osum:
        copy.wait_send()


def exchange_step(inv, trial, colloc, occupied, coords, weights):
    rows = trial.shape[0]
    hbm = pl.BlockSpec(memory_space=pl.ANY)
    vmem = pl.BlockSpec(memory_space=pltpu.VMEM)
    smem = pl.BlockSpec(memory_space=pltpu.SMEM)
    return pl.pallas_call(
        main_kernel,
        out_shape=jax.ShapeDtypeStruct((2, 6 * BLK, 2, NOCC), F32),
        in_specs=[smem, hbm, vmem, vmem, vmem, vmem, vmem],
        out_specs=vmem,
        scratch_shapes=[
            *[pltpu.VMEM((4, SIG + 1, BLK, BLK), BF16)] * 8,
            pltpu.VMEM((4, SIG + 1, BLK, BLK), BF16),
            pltpu.VMEM((2, 4, 4, BLK, 256), BF16),
            pltpu.VMEM((2, 4, 4, BLK, 256), BF16),
            pltpu.VMEM((2, 4) + inv.shape, jnp.int32),
            pltpu.SMEM((2, 4) + inv.shape, jnp.int32),
            pltpu.VMEM((4, BLK, BLK), F32),
            pltpu.VMEM((2, 12, BLK, 256), F32),
            pltpu.VMEM((2, 2, 3, BLK, 256), BF16),
            pltpu.VMEM((2, 2, 3, BLK, 256), BF16),
            pltpu.VMEM((16, rows, 2, NOCC), BF16),
            pltpu.VMEM((rows, 256), BF16),
            pltpu.VMEM((ROWS, rows), BF16),
            pltpu.VMEM((2, ROWS, 512), BF16),
            pltpu.VMEM((2, 2, ROWS, 512), BF16),
            pltpu.VMEM((2, ROWS, 512), F32),
            pltpu.VMEM((2, ROWS, 512), BF16),
            pltpu.VMEM((2, 2, ROWS, 512), BF16),
            pltpu.VMEM((2, ROWS, 256), BF16),
            pltpu.VMEM((2, ROWS, 256), BF16),
            pltpu.VMEM((ROWS, 256), BF16),
            pltpu.VMEM((ROWS, 2 * NOCC), F32),
            pltpu.VMEM((7, ROWS // 8, 2 * NOCC), F32),
            pltpu.VMEM((ROWS, 2 * NOCC), BF16),
            pltpu.SemaphoreType.DMA((16,)),
            pltpu.SemaphoreType.DMA((14,)),
            pltpu.SemaphoreType.DMA((14,)),
            pltpu.SemaphoreType.DMA((14,)),
            pltpu.SemaphoreType.DMA((14,)),
            pltpu.SemaphoreType.DMA((37,)),
            pltpu.SemaphoreType.DMA((37,)),
            pltpu.SemaphoreType.DMA((4,)),
            pltpu.SemaphoreType.DMA((4,)),
            pltpu.SemaphoreType.DMA,
        ],
        compiler_params=pltpu.CompilerParams(
            vmem_limit_bytes=63 << 20, collective_id=0, has_side_effects=True
        ),
        name="exchange_step",
    )(inv, trial, colloc, occupied, inv, coords, weights)


def place_of(ids, wanted):
    hit = ids[..., None, :] == wanted[..., :, None]
    where = jnp.arange(SIG, dtype=jnp.int32)
    return SIG + jnp.sum(jnp.where(hit, where - SIG, 0), axis=-1).astype(jnp.int32)


def on_device(trial, occupied, colloc, blocks, coords, weights):
    nblk = trial.shape[0] // BLK * lax.axis_size("ao")
    inv = place_of(blocks, jnp.arange(nblk, dtype=jnp.int32))
    inv = jnp.pad(inv, ((0, 4), (0, BLK - nblk)))
    return exchange_step(inv, trial, colloc, occupied, coords.transpose(1, 0, 2), weights)


def solution(mesh):
    in_specs = (
        P("ao", None, None, None),
        P("ao", None, None),
        P("grid", None, None),
        P("grid", None),
        P("grid", None, None),
        P("grid", None),
    )
    out_specs = P("ao", "grid", None, None)
    return jax.shard_map(
        on_device, mesh=mesh, in_specs=in_specs, out_specs=out_specs, check_vma=False
    )
```

```python
import functools
import jax
import jax.numpy as jnp
from jax import lax
from jax.experimental import pallas as pl
from jax.experimental.pallas import tpu as pltpu
from jax.sharding import PartitionSpec as P

BLK = 128
NOCC = 128
SIG = 12
F32 = jnp.float32
BF16 = jnp.bfloat16
MESH = pl.DeviceIdType.MESH
ROWS = 512


def coords_of():
    g = lax.axis_index("grid")
    a = lax.axis_index("ao")
    return g // 8, lax.rem(g // 2, 4), lax.rem(g, 2), a // 2, lax.rem(a, 2)


def device_at(zh, y, c, x, zl):
    return (zh * 8 + y * 2 + c, x * 2 + zl)


class GatherY:
    def __init__(self, own, slots, first, count, base, send, recv, tail=()):
        self.own, self.slots, self.base = own, slots, base
        self.send, self.recv, self.tail = send, recv, tail
        half = count // 2
        self.every = pl.ds(first, count)
        self.lo, self.hi = pl.ds(first, half), pl.ds(first + half, half)
        zh, y, c, x, zl = coords_of()
        self.right = device_at(zh, lax.rem(y + 1, 4), c, x, zl)
        self.left = device_at(zh, lax.rem(y + 3, 4), c, x, zl)
        self.twin = device_at(zh, y, 1 - c, x, zl)

    def at(self, n):
        own, slots, lo, hi, every = self.own, self.slots, self.lo, self.hi, self.every

        def o(b):
            return own.at[(b,) + self.tail]

        def s(i, slot, b):
            return slots(i, slot).at[(b,) + self.tail]

        src, dst, to = [
            (o(lo), s(0, 1, lo), self.right),
            (o(hi), s(0, 2, hi), self.left),
            (o(hi), s(0, 1, hi), self.right),
            (o(lo), s(0, 2, lo), self.left),
            (o(every), s(1, 0, every), self.twin),
            (s(0, 1, lo), s(0, 3, lo), self.right),
            (s(0, 2, hi), s(0, 3, hi), self.left),
            (s(0, 1, every), s(1, 1, every), self.twin),
            (s(0, 2, every), s(1, 2, every), self.twin),
            (s(0, 3, every), s(1, 3, every), self.twin),
        ][n]
        return remote(self.send, self.recv, self.base + n, src, dst, to)

    def start_first(self):
        for n in (0, 1):
            self.at(n).start()

    def start_second(self):
        for n in (2, 3, 4):
            self.at(n).start()

    def forward(self):
        for n in (0, 1):
            self.at(n).wait_recv()
            self.at(n + 5).start()

    def spread(self):
        for n in (2, 3):
            self.at(n).wait_recv()
            self.at(n + 5).start()

    def spread_opposite(self):
        for n in (5, 6):
            self.at(n).wait_recv()
        self.at(9).start()

    def arrived(self, *which):
        for n in which:
            self.at(n).wait_recv()

    def sent(self):
        for n in range(10):
            self.at(n).wait_send()


def remote(send, recv, n, src, dst, to):
    return pltpu.make_async_remote_copy(
        src_ref=src, dst_ref=dst, send_sem=send.at[n], recv_sem=recv.at[n],
        device_id=to, device_id_type=MESH,
    )


def greet(peers):
    barrier = pltpu.get_barrier_semaphore()
    for peer in peers:
        pl.semaphore_signal(barrier, inc=1, device_id=peer, device_id_type=MESH)
    pl.semaphore_wait(barrier, len(peers))


def rows_of(start, size):
    return pl.ds(pl.multiple_of(start, size), size)


def main_kernel(
    inv_ref, trial_ref, x_ref, occ_ref, place_ref, coords_ref, weights_ref, out_ref,
    x00, x01, x02, x03, x10, x11, x12, x13, xpad, e0, e1, places, table, kern, acc, give, got,
    buf, w, xloc, opp, part, own, rec1, rec2, zsend, zrec, lg, od, orec, og,
    load_sem, send, recv, osend, orecv, gsend, grecv, hsend, hrecv, local,
):
    zh, y, c, x, zl = coords_of()
    a = x * 2 + zl
    beyond = device_at(1 - zh, y, c, x, zl)
    right = device_at(zh, y, c, lax.rem(x + 1, 4), zl)
    left = device_at(zh, y, c, lax.rem(x + 3, 4), zl)
    across = device_at(zh, y, c, x, 1 - zl)
    order = [lax.rem(x + d, 4) for d in (2, 1, 3, 0)]

    def load(v):
        return pltpu.make_async_copy(trial_ref.at[:, v], buf.at[v], load_sem.at[v])

    for q in (0, 1):
        for dest in order:
            for t in range(2):
                load(dest * 4 + 2 * t + q).start()

    ao_peers = [(lax.axis_index("grid"), lax.rem(a + d, 8)) for d in range(1, 8)]
    grid_peers = [
        (device_at(zh, lax.rem(y + d, 4), c if same else 1 - c, x, zl), 0 if same else 1, slot)
        for d, slot in ((0, 0), (1, 1), (3, 2), (2, 3))
        for same in (True, False)
        if d or not same
    ]
    greet(ao_peers + [peer for peer, _, _ in grid_peers] + [beyond])

    def split(src):
        def some(k, _):
            k = pl.ds(pl.multiple_of(k * 256, 256), 256)
            both = src[k].astype(F32)
            w[k, :NOCC] = both[:, 0, :].astype(BF16)
            w[k, NOCC:] = both[:, 1, :].astype(BF16)
            return 0

        lax.fori_loop(0, w.shape[0] // 256, some, 0)

    zero = jnp.zeros((BLK, BLK), BF16)
    for b in range(4):
        for n in range(SIG):
            xpad[b, n] = x_ref[b, :, n * BLK : (n + 1) * BLK]
        xpad[b, SIG] = zero
    nloc = xloc.shape[1] // BLK
    for b in range(4):
        for l in range(nloc):
            xloc[b * BLK : (b + 1) * BLK, l * BLK : (l + 1) * BLK] = xpad[b, inv_ref[b, a * nloc + l]]

    split(occ_ref)
    od[...] = jnp.dot(xloc[...], w[...], preferred_element_type=F32)
    osum = [
        remote(osend, orecv, d - 1, od.at[rows_of(lax.rem(a + d, 8) * 64, 64)], orec.at[d - 1], ao_peers[d - 1])
        for d in range(1, 8)
    ]
    for copy in osum:
        copy.start()

    xs = [[x00, x01, x02, x03], [x10, x11, x12, x13]]
    es = [e0, e1]
    gx = GatherY(x00, lambda i, slot: xs[i][slot], 0, 4, 0, gsend, grecv, (pl.ds(0, SIG),))
    ge = [
        GatherY(es[q].at[0, 0], lambda i, slot, q=q: es[q].at[i, slot], 0, 4, 10 + 10 * q, gsend, grecv)
        for q in (0, 1)
    ]
    tables = [
        remote(gsend, grecv, 30 + n, place_ref, places.at[i, slot], peer)
        for n, (peer, i, slot) in enumerate(grid_peers)
    ]
    for copy in tables:
        copy.start()
    places[0, 0] = place_ref[...]
    for i in range(2):
        for slot in range(4):
            for b in range(4):
                xs[i][slot][b, SIG] = zero

    def densities(dest, q, store):
        def one(t, _):
            v = dest * 4 + 2 * t + q
            load(v).wait()
            split(buf.at[v])
            store(
                pl.ds(pl.multiple_of(t * 256, 256), 256),
                jnp.dot(xloc[...], w[...], preferred_element_type=F32),
            )
            return 0

        lax.fori_loop(0, 2, one, 0)

    lo, hi = pl.ds(0, 256), pl.ds(256, 256)
    halves = (lo, hi)
    sides = (right, left)
    to_opp = [
        [remote(send, recv, 2 * q + k, opp.at[q, halves[k]], rec1.at[q, halves[k]], sides[k]) for k in (0, 1)]
        for q in (0, 1)
    ]
    to_side = [
        [
            [
                remote(send, recv, 4 + 4 * q + 2 * k + h, part.at[k, q, halves[h]], rec2.at[k, q, halves[h]], sides[k])
                for h in (0, 1)
            ]
            for k in (0, 1)
        ]
        for q in (0, 1)
    ]
    to_pair = [remote(send, recv, 12 + q, zsend.at[q], zrec.at[q], across) for q in (0, 1)]

    def dens_opp(q):
        def store(cols, value):
            opp[q, :, cols] = value.astype(BF16)

        densities(order[0], q, store)
        for copy in to_opp[q]:
            copy.start()

    def dens_side(k, q):
        def store(cols, value):
            own[q, halves[k], cols] = value[256 * k : 256 * k + 256]
            part[k, q, halves[1 - k], cols] = value[256 - 256 * k : 512 - 256 * k].astype(BF16)

        densities(order[1 + k], q, store)
        to_side[q][k][1 - k].start()

    def add_side(k, q):
        to_opp[q][k].wait_recv()

        def some(i, _):
            r = rows_of(256 * k + i * 16, 16)
            part[k, q, r] = (own[q, r] + rec1[q, r].astype(F32)).astype(BF16)
            return 0

        lax.fori_loop(0, 16, some, 0)
        to_side[q][k][k].start()

    def dens_own(q):
        def store(cols, value):
            own[q, :, cols] = value

        densities(order[3], q, store)

    theirs = pl.ds(pl.multiple_of((1 - zl) * 256, 256), 256)
    mine = pl.ds(pl.multiple_of(zl * 256, 256), 256)

    def total(q, r, cols):
        return own[q, r, cols] + rec2[0, q, r, cols].astype(F32) + rec2[1, q, r, cols].astype(F32)

    def to_z(q):
        for k in (0, 1):
            for h in (0, 1):
                to_side[q][k][h].wait_recv()

        def some(i, _):
            r = rows_of(i * 32, 32)
            zsend[q, r] = total(q, r, theirs).astype(BF16)
            return 0

        lax.fori_loop(0, 16, some, 0)
        to_pair[q].start()

    def pair(q):
        to_pair[q].wait_recv()

        def some(i, _):
            r = rows_of(i * 32, 32)
            lg[r] = (total(q, r, mine) + zrec[q, r].astype(F32)).astype(BF16)
            return 0

        lax.fori_loop(0, 16, some, 0)
        for b in range(4):
            rows = pl.ds(b * BLK, BLK)
            ore = og[rows, :NOCC].astype(F32)
            oim = og[rows, NOCC:].astype(F32)
            ww = jnp.concatenate(
                [
                    jnp.concatenate([ore, oim], axis=1),
                    jnp.concatenate([-oim, ore], axis=1),
                ],
                axis=0,
            ).astype(BF16)
            rho = lax.dot_general(
                lg[rows], ww, (((1,), (1,)), ((), ())), preferred_element_type=F32
            )
            m = (rho * jnp.concatenate([kern[b], kern[b]], axis=1)).astype(BF16)
            es[q][0, 0, b] = jnp.dot(m, ww, preferred_element_type=F32).astype(BF16)
        ge[q].start_first()
        ge[q].start_second()

    first = (y * 2 + c) * 6
    GROUP = 3

    def panel(i, slot, q, start, stop, fresh=False):
        def row(n, _):
            lines = []
            for k in range(GROUP):
                r = n * GROUP + k
                block = jnp.where(r < 6, (1 - zh) * 48 + first + r, zh * 48 + first + r - 6)
                lines.append(
                    jnp.concatenate([xs[i][slot][b, table[i, slot, b, block]] for b in range(4)], axis=1)
                )
            value = jnp.dot(
                jnp.concatenate(lines, axis=0), es[q][i, slot].reshape(4 * BLK, 256),
                preferred_element_type=F32,
            ).reshape(GROUP, BLK, 256)
            at = pl.ds(n * GROUP, GROUP)
            acc[q, at] = value if fresh else acc[q, at] + value
            return 0

        lax.fori_loop(start, stop, row, 0)

    over = [
        [remote(hsend, hrecv, 2 * q + n, give.at[q, n], got.at[q, n], beyond) for n in range(2)]
        for q in (0, 1)
    ]

    def middle(q):
        ge[q].spread_opposite()
        ge[q].arrived(4)
        panel(1, 0, q, 0, 4)
        panel(0, 1, q, 0, 4)
        panel(0, 2, q, 0, 4)
        ge[q].arrived(7, 8)
        panel(1, 1, q, 0, 4)
        panel(1, 2, q, 0, 4)
        panel(0, 3, q, 0, 4)

    def last(q):
        ge[q].arrived(9)
        for n in (0, 1):
            panel(1, 3, q, n, n + 1)
            give[q, n] = acc[q, 3 * n : 3 * n + 3].astype(BF16)
            over[q][n].start()
        panel(1, 3, q, 2, 4)

    def finish(q):
        for r in range(6):
            if r % 3 == 0:
                over[q][r // 3].wait_recv()
            for k in range(2):
                cols = slice(k * 128, k * 128 + 128)
                out_ref[q, r * BLK : (r + 1) * BLK, k, :] = acc[q, 6 + r, :, cols] + got[
                    q, r // 3, r % 3, :, cols
                ].astype(F32)

    dens_opp(0)
    for b in range(4):
        for n in range(SIG):
            x00[b, n] = x_ref[b, :, n * BLK : (n + 1) * BLK].T
    gx.start_first()
    dens_side(0, 0)
    for copy in osum:
        copy.wait_recv()
    mine64 = rows_of(a * 64, 64)
    og[mine64] = (od[mine64] + sum(orec[n] for n in range(7))).astype(BF16)
    ogat = [
        remote(osend, orecv, 7 + d - 1, og.at[mine64], og.at[mine64], ao_peers[d - 1])
        for d in range(1, 8)
    ]
    for copy in ogat:
        copy.start()
    add_side(0, 0)
    dens_side(1, 0)
    add_side(1, 0)
    dens_own(0)
    dens_opp(1)
    dens_side(0, 1)
    dens_side(1, 1)
    add_side(0, 1)
    add_side(1, 1)
    gx.forward()
    gx.start_second()
    to_z(0)

    def spread_row(row):
        return jnp.broadcast_to(row, (BLK, BLK))

    for b in range(4):
        square = None
        for k in range(3):
            along = spread_row(coords_ref[k, b : b + 1, :])
            differ = along.T - along
            square = differ * differ if square is None else square + differ * differ
        quad = spread_row(weights_ref[b : b + 1, :])
        kern[b] = quad.T * quad / jnp.sqrt(square + 0.25)
    for copy in tables + ogat:
        copy.wait_recv()
    fill = pltpu.make_async_copy(places, table, local)
    fill.start()
    pair(0)
    fill.wait()
    dens_own(1)
    panel(0, 0, 0, 0, 4, fresh=True)
    to_z(1)
    ge[0].forward()
    ge[0].spread()
    pair(1)
    gx.spread()
    gx.spread_opposite()
    gx.arrived(4, 7, 8)
    middle(0)
    ge[1].forward()
    ge[1].spread()
    gx.arrived(9)
    last(0)
    panel(0, 0, 1, 0, 4, fresh=True)
    middle(1)
    last(1)
    finish(0)
    finish(1)
    for gather in [gx] + ge:
        gather.sent()
    for q in (0, 1):
        for copy in to_opp[q] + to_side[q][0] + to_side[q][1] + over[q] + [to_pair[q]]:
            copy.wait_send()
    for copy in tables + ogat + osum:
        copy.wait_send()


def exchange_step(inv, trial, colloc, occupied, coords, weights):
    rows = trial.shape[0]
    hbm = pl.BlockSpec(memory_space=pl.ANY)
    vmem = pl.BlockSpec(memory_space=pltpu.VMEM)
    smem = pl.BlockSpec(memory_space=pltpu.SMEM)
    return pl.pallas_call(
        main_kernel,
        out_shape=jax.ShapeDtypeStruct((2, 6 * BLK, 2, NOCC), F32),
        in_specs=[smem, hbm, vmem, vmem, vmem, vmem, vmem],
        out_specs=vmem,
        scratch_shapes=[
            *[pltpu.VMEM((4, SIG + 1, BLK, BLK), BF16)] * 8,
            pltpu.VMEM((4, SIG + 1, BLK, BLK), BF16),
            pltpu.VMEM((2, 4, 4, BLK, 256), BF16),
            pltpu.VMEM((2, 4, 4, BLK, 256), BF16),
            pltpu.VMEM((2, 4) + inv.shape, jnp.int32),
            pltpu.SMEM((2, 4) + inv.shape, jnp.int32),
            pltpu.VMEM((4, BLK, BLK), F32),
            pltpu.VMEM((2, 12, BLK, 256), F32),
            pltpu.VMEM((2, 2, 3, BLK, 256), BF16),
            pltpu.VMEM((2, 2, 3, BLK, 256), BF16),
            pltpu.VMEM((16, rows, 2, NOCC), BF16),
            pltpu.VMEM((rows, 256), BF16),
            pltpu.VMEM((ROWS, rows), BF16),
            pltpu.VMEM((2, ROWS, 512), BF16),
            pltpu.VMEM((2, 2, ROWS, 512), BF16),
            pltpu.VMEM((2, ROWS, 512), F32),
            pltpu.VMEM((2, ROWS, 512), BF16),
            pltpu.VMEM((2, 2, ROWS, 512), BF16),
            pltpu.VMEM((2, ROWS, 256), BF16),
            pltpu.VMEM((2, ROWS, 256), BF16),
            pltpu.VMEM((ROWS, 256), BF16),
            pltpu.VMEM((ROWS, 2 * NOCC), F32),
            pltpu.VMEM((7, ROWS // 8, 2 * NOCC), F32),
            pltpu.VMEM((ROWS, 2 * NOCC), BF16),
            pltpu.SemaphoreType.DMA((16,)),
            pltpu.SemaphoreType.DMA((14,)),
            pltpu.SemaphoreType.DMA((14,)),
            pltpu.SemaphoreType.DMA((14,)),
            pltpu.SemaphoreType.DMA((14,)),
            pltpu.SemaphoreType.DMA((37,)),
            pltpu.SemaphoreType.DMA((37,)),
            pltpu.SemaphoreType.DMA((4,)),
            pltpu.SemaphoreType.DMA((4,)),
            pltpu.SemaphoreType.DMA,
        ],
        compiler_params=pltpu.CompilerParams(
            vmem_limit_bytes=63 << 20, collective_id=0, has_side_effects=True
        ),
        name="exchange_step",
    )(inv, trial, colloc, occupied, inv, coords, weights)


def place_of(ids, wanted):
    hit = ids[..., None, :] == wanted[..., :, None]
    where = jnp.arange(SIG, dtype=jnp.int32)
    return SIG + jnp.sum(jnp.where(hit, where - SIG, 0), axis=-1).astype(jnp.int32)


def on_device(trial, occupied, colloc, blocks, coords, weights):
    nblk = trial.shape[0] // BLK * lax.axis_size("ao")
    inv = place_of(blocks, jnp.arange(nblk, dtype=jnp.int32))
    inv = jnp.pad(inv, ((0, 4), (0, BLK - nblk)))
    return exchange_step(inv, trial, colloc, occupied, coords.transpose(1, 0, 2), weights)


def solution(mesh):
    in_specs = (
        P("ao", None, None, None),
        P("ao", None, None),
        P("grid", None, None),
        P("grid", None),
        P("grid", None, None),
        P("grid", None),
    )
    out_specs = P("ao", "grid", None, None)
    return jax.shard_map(
        on_device, mesh=mesh, in_specs=in_specs, out_specs=out_specs, check_vma=False
    )
```

```python
import functools
import jax
import jax.numpy as jnp
from jax import lax
from jax.experimental import pallas as pl
from jax.experimental.pallas import tpu as pltpu
from jax.sharding import PartitionSpec as P

BLK = 128
NOCC = 128
SIG = 12
F32 = jnp.float32
BF16 = jnp.bfloat16
MESH = pl.DeviceIdType.MESH
ROWS = 512


def coords_of():
    g = lax.axis_index("grid")
    a = lax.axis_index("ao")
    return g // 8, lax.rem(g // 2, 4), lax.rem(g, 2), a // 2, lax.rem(a, 2)


def device_at(zh, y, c, x, zl):
    return (zh * 8 + y * 2 + c, x * 2 + zl)


class GatherY:
    def __init__(self, own, slots, first, count, base, send, recv, tail=()):
        self.own, self.slots, self.base = own, slots, base
        self.send, self.recv, self.tail = send, recv, tail
        half = count // 2
        self.every = pl.ds(first, count)
        self.lo, self.hi = pl.ds(first, half), pl.ds(first + half, half)
        zh, y, c, x, zl = coords_of()
        self.right = device_at(zh, lax.rem(y + 1, 4), c, x, zl)
        self.left = device_at(zh, lax.rem(y + 3, 4), c, x, zl)
        self.twin = device_at(zh, y, 1 - c, x, zl)

    def at(self, n):
        own, slots, lo, hi, every = self.own, self.slots, self.lo, self.hi, self.every

        def o(b):
            return own.at[(b,) + self.tail]

        def s(i, slot, b):
            return slots(i, slot).at[(b,) + self.tail]

        src, dst, to = [
            (o(lo), s(0, 1, lo), self.right),
            (o(hi), s(0, 2, hi), self.left),
            (o(hi), s(0, 1, hi), self.right),
            (o(lo), s(0, 2, lo), self.left),
            (o(every), s(1, 0, every), self.twin),
            (s(0, 1, lo), s(0, 3, lo), self.right),
            (s(0, 2, hi), s(0, 3, hi), self.left),
            (s(0, 1, every), s(1, 1, every), self.twin),
            (s(0, 2, every), s(1, 2, every), self.twin),
            (s(0, 3, every), s(1, 3, every), self.twin),
        ][n]
        return remote(self.send, self.recv, self.base + n, src, dst, to)

    def start_first(self):
        for n in (0, 1):
            self.at(n).start()

    def start_second(self):
        for n in (2, 3, 4):
            self.at(n).start()

    def forward(self):
        for n in (0, 1):
            self.at(n).wait_recv()
            self.at(n + 5).start()

    def spread(self):
        for n in (2, 3):
            self.at(n).wait_recv()
            self.at(n + 5).start()

    def spread_opposite(self):
        for n in (5, 6):
            self.at(n).wait_recv()
        self.at(9).start()

    def arrived(self, *which):
        for n in which:
            self.at(n).wait_recv()

    def sent(self):
        for n in range(10):
            self.at(n).wait_send()


def remote(send, recv, n, src, dst, to):
    return pltpu.make_async_remote_copy(
        src_ref=src, dst_ref=dst, send_sem=send.at[n], recv_sem=recv.at[n],
        device_id=to, device_id_type=MESH,
    )


def greet(peers):
    barrier = pltpu.get_barrier_semaphore()
    for peer in peers:
        pl.semaphore_signal(barrier, inc=1, device_id=peer, device_id_type=MESH)
    pl.semaphore_wait(barrier, len(peers))


def rows_of(start, size):
    return pl.ds(pl.multiple_of(start, size), size)


def main_kernel(
    inv_ref, trial_ref, x_ref, occ_ref, place_ref, coords_ref, weights_ref, out_ref,
    x00, x01, x02, x03, x10, x11, x12, x13, xpad, e0, e1, places, table, kern, acc, give, got,
    buf, w, xloc, opp, part, own, rec1, rec2, zsend, zrec, lg, od, orec, og,
    load_sem, send, recv, osend, orecv, gsend, grecv, hsend, hrecv, local,
):
    zh, y, c, x, zl = coords_of()
    a = x * 2 + zl
    beyond = device_at(1 - zh, y, c, x, zl)
    right = device_at(zh, y, c, lax.rem(x + 1, 4), zl)
    left = device_at(zh, y, c, lax.rem(x + 3, 4), zl)
    across = device_at(zh, y, c, x, 1 - zl)
    order = [lax.rem(x + d, 4) for d in (2, 1, 3, 0)]

    def load(v):
        return pltpu.make_async_copy(trial_ref.at[:, v], buf.at[v], load_sem.at[v])

    for q in (0, 1):
        for dest in order:
            for t in range(2):
                load(dest * 4 + 2 * t + q).start()

    ao_peers = [(lax.axis_index("grid"), lax.rem(a + d, 8)) for d in range(1, 8)]
    grid_peers = [
        (device_at(zh, lax.rem(y + d, 4), c if same else 1 - c, x, zl), 0 if same else 1, slot)
        for d, slot in ((0, 0), (1, 1), (3, 2), (2, 3))
        for same in (True, False)
        if d or not same
    ]
    greet(ao_peers + [peer for peer, _, _ in grid_peers] + [beyond])

    xs = [[x00, x01, x02, x03], [x10, x11, x12, x13]]
    gx = GatherY(x00, lambda i, slot: xs[i][slot], 0, 4, 0, gsend, grecv, (pl.ds(0, SIG),))
    for b in range(4):
        for n in range(SIG):
            x00[b, n] = x_ref[b, :, n * BLK : (n + 1) * BLK].T
    gx.start_first()

    def split(src):
        def some(k, _):
            k = pl.ds(pl.multiple_of(k * 256, 256), 256)
            both = src[k].astype(F32)
            w[k, :NOCC] = both[:, 0, :].astype(BF16)
            w[k, NOCC:] = both[:, 1, :].astype(BF16)
            return 0

        lax.fori_loop(0, w.shape[0] // 256, some, 0)

    zero = jnp.zeros((BLK, BLK), BF16)
    for b in range(4):
        for n in range(SIG):
            xpad[b, n] = x_ref[b, :, n * BLK : (n + 1) * BLK]
        xpad[b, SIG] = zero
    nloc = xloc.shape[1] // BLK
    for b in range(4):
        for l in range(nloc):
            xloc[b * BLK : (b + 1) * BLK, l * BLK : (l + 1) * BLK] = xpad[b, inv_ref[b, a * nloc + l]]

    split(occ_ref)
    od[...] = jnp.dot(xloc[...], w[...], preferred_element_type=F32)
    osum = [
        remote(osend, orecv, d - 1, od.at[rows_of(lax.rem(a + d, 8) * 64, 64)], orec.at[d - 1], ao_peers[d - 1])
        for d in range(1, 8)
    ]
    for copy in osum:
        copy.start()

    es = [e0, e1]
    ge = [
        GatherY(es[q].at[0, 0], lambda i, slot, q=q: es[q].at[i, slot], 0, 4, 10 + 10 * q, gsend, grecv)
        for q in (0, 1)
    ]
    tables = [
        remote(gsend, grecv, 30 + n, place_ref, places.at[i, slot], peer)
        for n, (peer, i, slot) in enumerate(grid_peers)
    ]
    for copy in tables:
        copy.start()
    places[0, 0] = place_ref[...]
    for i in range(2):
        for slot in range(4):
            for b in range(4):
                xs[i][slot][b, SIG] = zero

    def densities(dest, q, store):
        def one(t, _):
            v = dest * 4 + 2 * t + q
            load(v).wait()
            split(buf.at[v])
            store(
                pl.ds(pl.multiple_of(t * 256, 256), 256),
                jnp.dot(xloc[...], w[...], preferred_element_type=F32),
            )
            return 0

        lax.fori_loop(0, 2, one, 0)

    lo, hi = pl.ds(0, 256), pl.ds(256, 256)
    halves = (lo, hi)
    sides = (right, left)
    to_opp = [
        [remote(send, recv, 2 * q + k, opp.at[q, halves[k]], rec1.at[q, halves[k]], sides[k]) for k in (0, 1)]
        for q in (0, 1)
    ]
    to_side = [
        [
            [
                remote(send, recv, 4 + 4 * q + 2 * k + h, part.at[k, q, halves[h]], rec2.at[k, q, halves[h]], sides[k])
                for h in (0, 1)
            ]
            for k in (0, 1)
        ]
        for q in (0, 1)
    ]
    to_pair = [remote(send, recv, 12 + q, zsend.at[q], zrec.at[q], across) for q in (0, 1)]

    def dens_opp(q):
        def store(cols, value):
            opp[q, :, cols] = value.astype(BF16)

        densities(order[0], q, store)
        for copy in to_opp[q]:
            copy.start()

    def dens_side(k, q):
        def store(cols, value):
            own[q, halves[k], cols] = value[256 * k : 256 * k + 256]
            part[k, q, halves[1 - k], cols] = value[256 - 256 * k : 512 - 256 * k].astype(BF16)

        densities(order[1 + k], q, store)
        to_side[q][k][1 - k].start()

    def add_side(k, q):
        to_opp[q][k].wait_recv()

        def some(i, _):
            r = rows_of(256 * k + i * 16, 16)
            part[k, q, r] = (own[q, r] + rec1[q, r].astype(F32)).astype(BF16)
            return 0

        lax.fori_loop(0, 16, some, 0)
        to_side[q][k][k].start()

    def dens_own(q):
        def store(cols, value):
            own[q, :, cols] = value

        densities(order[3], q, store)

    theirs = pl.ds(pl.multiple_of((1 - zl) * 256, 256), 256)
    mine = pl.ds(pl.multiple_of(zl * 256, 256), 256)

    def total(q, r, cols):
        return own[q, r, cols] + rec2[0, q, r, cols].astype(F32) + rec2[1, q, r, cols].astype(F32)

    def to_z(q):
        for k in (0, 1):
            for h in (0, 1):
                to_side[q][k][h].wait_recv()

        def some(i, _):
            r = rows_of(i * 32, 32)
            zsend[q, r] = total(q, r, theirs).astype(BF16)
            return 0

        lax.fori_loop(0, 16, some, 0)
        to_pair[q].start()

    def pair(q):
        to_pair[q].wait_recv()

        def some(i, _):
            r = rows_of(i * 32, 32)
            lg[r] = (total(q, r, mine) + zrec[q, r].astype(F32)).astype(BF16)
            return 0

        lax.fori_loop(0, 16, some, 0)
        for b in range(4):
            rows = pl.ds(b * BLK, BLK)
            ore = og[rows, :NOCC].astype(F32)
            oim = og[rows, NOCC:].astype(F32)
            ww = jnp.concatenate(
                [
                    jnp.concatenate([ore, oim], axis=1),
                    jnp.concatenate([-oim, ore], axis=1),
                ],
                axis=0,
            ).astype(BF16)
            rho = lax.dot_general(
                lg[rows], ww, (((1,), (1,)), ((), ())), preferred_element_type=F32
            )
            m = (rho * jnp.concatenate([kern[b], kern[b]], axis=1)).astype(BF16)
            es[q][0, 0, b] = jnp.dot(m, ww, preferred_element_type=F32).astype(BF16)
        ge[q].start_first()
        ge[q].start_second()

    first = (y * 2 + c) * 6
    GROUP = 3

    def panel(i, slot, q, start, stop, fresh=False):
        def row(n, _):
            lines = []
            for k in range(GROUP):
                r = n * GROUP + k
                block = jnp.where(r < 6, (1 - zh) * 48 + first + r, zh * 48 + first + r - 6)
                lines.append(
                    jnp.concatenate([xs[i][slot][b, table[i, slot, b, block]] for b in range(4)], axis=1)
                )
            value = jnp.dot(
                jnp.concatenate(lines, axis=0), es[q][i, slot].reshape(4 * BLK, 256),
                preferred_element_type=F32,
            ).reshape(GROUP, BLK, 256)
            at = pl.ds(n * GROUP, GROUP)
            acc[q, at] = value if fresh else acc[q, at] + value
            return 0

        lax.fori_loop(start, stop, row, 0)

    over = [
        [remote(hsend, hrecv, 2 * q + n, give.at[q, n], got.at[q, n], beyond) for n in range(2)]
        for q in (0, 1)
    ]

    def middle(q):
        ge[q].spread_opposite()
        ge[q].arrived(4)
        panel(1, 0, q, 0, 4)
        panel(0, 1, q, 0, 4)
        panel(0, 2, q, 0, 4)
        ge[q].arrived(7, 8)
        panel(1, 1, q, 0, 4)
        panel(1, 2, q, 0, 4)
        panel(0, 3, q, 0, 4)

    def last(q):
        ge[q].arrived(9)
        for n in (0, 1):
            panel(1, 3, q, n, n + 1)
            give[q, n] = acc[q, 3 * n : 3 * n + 3].astype(BF16)
            over[q][n].start()
        panel(1, 3, q, 2, 4)

    def finish(q):
        for r in range(6):
            if r % 3 == 0:
                over[q][r // 3].wait_recv()
            for k in range(2):
                cols = slice(k * 128, k * 128 + 128)
                out_ref[q, r * BLK : (r + 1) * BLK, k, :] = acc[q, 6 + r, :, cols] + got[
                    q, r // 3, r % 3, :, cols
                ].astype(F32)

    dens_opp(0)
    dens_side(0, 0)
    for copy in osum:
        copy.wait_recv()
    mine64 = rows_of(a * 64, 64)
    og[mine64] = (od[mine64] + sum(orec[n] for n in range(7))).astype(BF16)
    ogat = [
        remote(osend, orecv, 7 + d - 1, og.at[mine64], og.at[mine64], ao_peers[d - 1])
        for d in range(1, 8)
    ]
    for copy in ogat:
        copy.start()
    add_side(0, 0)
    dens_side(1, 0)
    add_side(1, 0)
    gx.forward()
    gx.start_second()
    dens_own(0)
    dens_opp(1)
    dens_side(0, 1)
    dens_side(1, 1)
    add_side(0, 1)
    add_side(1, 1)
    to_z(0)

    def spread_row(row):
        return jnp.broadcast_to(row, (BLK, BLK))

    for b in range(4):
        square = None
        for k in range(3):
            along = spread_row(coords_ref[k, b : b + 1, :])
            differ = along.T - along
            square = differ * differ if square is None else square + differ * differ
        quad = spread_row(weights_ref[b : b + 1, :])
        kern[b] = quad.T * quad / jnp.sqrt(square + 0.25)
    for copy in tables + ogat:
        copy.wait_recv()
    fill = pltpu.make_async_copy(places, table, local)
    fill.start()
    pair(0)
    fill.wait()
    dens_own(1)
    panel(0, 0, 0, 0, 4, fresh=True)
    to_z(1)
    ge[0].forward()
    ge[0].spread()
    pair(1)
    gx.spread()
    gx.spread_opposite()
    gx.arrived(4, 7, 8)
    middle(0)
    ge[1].forward()
    ge[1].spread()
    gx.arrived(9)
    last(0)
    panel(0, 0, 1, 0, 4, fresh=True)
    middle(1)
    last(1)
    finish(0)
    finish(1)
    for gather in [gx] + ge:
        gather.sent()
    for q in (0, 1):
        for copy in to_opp[q] + to_side[q][0] + to_side[q][1] + over[q] + [to_pair[q]]:
            copy.wait_send()
    for copy in tables + ogat + osum:
        copy.wait_send()


def exchange_step(inv, trial, colloc, occupied, coords, weights):
    rows = trial.shape[0]
    hbm = pl.BlockSpec(memory_space=pl.ANY)
    vmem = pl.BlockSpec(memory_space=pltpu.VMEM)
    smem = pl.BlockSpec(memory_space=pltpu.SMEM)
    return pl.pallas_call(
        main_kernel,
        out_shape=jax.ShapeDtypeStruct((2, 6 * BLK, 2, NOCC), F32),
        in_specs=[smem, hbm, vmem, vmem, vmem, vmem, vmem],
        out_specs=vmem,
        scratch_shapes=[
            *[pltpu.VMEM((4, SIG + 1, BLK, BLK), BF16)] * 8,
            pltpu.VMEM((4, SIG + 1, BLK, BLK), BF16),
            pltpu.VMEM((2, 4, 4, BLK, 256), BF16),
            pltpu.VMEM((2, 4, 4, BLK, 256), BF16),
            pltpu.VMEM((2, 4) + inv.shape, jnp.int32),
            pltpu.SMEM((2, 4) + inv.shape, jnp.int32),
            pltpu.VMEM((4, BLK, BLK), F32),
            pltpu.VMEM((2, 12, BLK, 256), F32),
            pltpu.VMEM((2, 2, 3, BLK, 256), BF16),
            pltpu.VMEM((2, 2, 3, BLK, 256), BF16),
            pltpu.VMEM((16, rows, 2, NOCC), BF16),
            pltpu.VMEM((rows, 256), BF16),
            pltpu.VMEM((ROWS, rows), BF16),
            pltpu.VMEM((2, ROWS, 512), BF16),
            pltpu.VMEM((2, 2, ROWS, 512), BF16),
            pltpu.VMEM((2, ROWS, 512), F32),
            pltpu.VMEM((2, ROWS, 512), BF16),
            pltpu.VMEM((2, 2, ROWS, 512), BF16),
            pltpu.VMEM((2, ROWS, 256), BF16),
            pltpu.VMEM((2, ROWS, 256), BF16),
            pltpu.VMEM((ROWS, 256), BF16),
            pltpu.VMEM((ROWS, 2 * NOCC), F32),
            pltpu.VMEM((7, ROWS // 8, 2 * NOCC), F32),
            pltpu.VMEM((ROWS, 2 * NOCC), BF16),
            pltpu.SemaphoreType.DMA((16,)),
            pltpu.SemaphoreType.DMA((14,)),
            pltpu.SemaphoreType.DMA((14,)),
            pltpu.SemaphoreType.DMA((14,)),
            pltpu.SemaphoreType.DMA((14,)),
            pltpu.SemaphoreType.DMA((37,)),
            pltpu.SemaphoreType.DMA((37,)),
            pltpu.SemaphoreType.DMA((4,)),
            pltpu.SemaphoreType.DMA((4,)),
            pltpu.SemaphoreType.DMA,
        ],
        compiler_params=pltpu.CompilerParams(
            vmem_limit_bytes=63 << 20, collective_id=0, has_side_effects=True
        ),
        name="exchange_step",
    )(inv, trial, colloc, occupied, inv, coords, weights)


def place_of(ids, wanted):
    hit = ids[..., None, :] == wanted[..., :, None]
    where = jnp.arange(SIG, dtype=jnp.int32)
    return SIG + jnp.sum(jnp.where(hit, where - SIG, 0), axis=-1).astype(jnp.int32)


def on_device(trial, occupied, colloc, blocks, coords, weights):
    nblk = trial.shape[0] // BLK * lax.axis_size("ao")
    inv = place_of(blocks, jnp.arange(nblk, dtype=jnp.int32))
    inv = jnp.pad(inv, ((0, 4), (0, BLK - nblk)))
    return exchange_step(inv, trial, colloc, occupied, coords.transpose(1, 0, 2), weights)


def solution(mesh):
    in_specs = (
        P("ao", None, None, None),
        P("ao", None, None),
        P("grid", None, None),
        P("grid", None),
        P("grid", None, None),
        P("grid", None),
    )
    out_specs = P("ao", "grid", None, None)
    return jax.shard_map(
        on_device, mesh=mesh, in_specs=in_specs, out_specs=out_specs, check_vma=False
    )
```

```python
import functools
import jax
import jax.numpy as jnp
from jax import lax
from jax.experimental import pallas as pl
from jax.experimental.pallas import tpu as pltpu
from jax.sharding import PartitionSpec as P

BLK = 128
NOCC = 128
SIG = 12
F32 = jnp.float32
BF16 = jnp.bfloat16
MESH = pl.DeviceIdType.MESH
ROWS = 512


def coords_of():
    g = lax.axis_index("grid")
    a = lax.axis_index("ao")
    return g // 8, lax.rem(g // 2, 4), lax.rem(g, 2), a // 2, lax.rem(a, 2)


def device_at(zh, y, c, x, zl):
    return (zh * 8 + y * 2 + c, x * 2 + zl)


class GatherY:
    def __init__(self, own, slots, first, count, base, send, recv, tail=()):
        self.own, self.slots, self.base = own, slots, base
        self.send, self.recv, self.tail = send, recv, tail
        half = count // 2
        self.every = pl.ds(first, count)
        self.lo, self.hi = pl.ds(first, half), pl.ds(first + half, half)
        zh, y, c, x, zl = coords_of()
        self.right = device_at(zh, lax.rem(y + 1, 4), c, x, zl)
        self.left = device_at(zh, lax.rem(y + 3, 4), c, x, zl)
        self.twin = device_at(zh, y, 1 - c, x, zl)

    def at(self, n):
        own, slots, lo, hi, every = self.own, self.slots, self.lo, self.hi, self.every

        def o(b):
            return own.at[(b,) + self.tail]

        def s(i, slot, b):
            return slots(i, slot).at[(b,) + self.tail]

        src, dst, to = [
            (o(lo), s(0, 1, lo), self.right),
            (o(hi), s(0, 2, hi), self.left),
            (o(hi), s(0, 1, hi), self.right),
            (o(lo), s(0, 2, lo), self.left),
            (o(every), s(1, 0, every), self.twin),
            (s(0, 1, lo), s(0, 3, lo), self.right),
            (s(0, 2, hi), s(0, 3, hi), self.left),
            (s(0, 1, every), s(1, 1, every), self.twin),
            (s(0, 2, every), s(1, 2, every), self.twin),
            (s(0, 3, every), s(1, 3, every), self.twin),
        ][n]
        return remote(self.send, self.recv, self.base + n, src, dst, to)

    def start_first(self):
        for n in (0, 1):
            self.at(n).start()

    def start_second(self):
        for n in (2, 3, 4):
            self.at(n).start()

    def forward(self):
        for n in (0, 1):
            self.at(n).wait_recv()
            self.at(n + 5).start()

    def spread(self):
        for n in (2, 3):
            self.at(n).wait_recv()
            self.at(n + 5).start()

    def spread_opposite(self):
        for n in (5, 6):
            self.at(n).wait_recv()
        self.at(9).start()

    def arrived(self, *which):
        for n in which:
            self.at(n).wait_recv()

    def sent(self):
        for n in range(10):
            self.at(n).wait_send()


def remote(send, recv, n, src, dst, to):
    return pltpu.make_async_remote_copy(
        src_ref=src, dst_ref=dst, send_sem=send.at[n], recv_sem=recv.at[n],
        device_id=to, device_id_type=MESH,
    )


def greet(peers):
    barrier = pltpu.get_barrier_semaphore()
    for peer in peers:
        pl.semaphore_signal(barrier, inc=1, device_id=peer, device_id_type=MESH)
    pl.semaphore_wait(barrier, len(peers))


def rows_of(start, size):
    return pl.ds(pl.multiple_of(start, size), size)


def main_kernel(
    inv_ref, trial_ref, x_ref, occ_ref, place_ref, coords_ref, weights_ref, out_ref,
    x00, x01, x02, x03, x10, x11, x12, x13, xpad, e0, e1, places, table, kern, acc, give, got,
    buf, w, xloc, opp, part, own, rec1, rec2, zsend, zrec, lg, od, orec, og,
    load_sem, send, recv, osend, orecv, gsend, grecv, hsend, hrecv, local,
):
    zh, y, c, x, zl = coords_of()
    a = x * 2 + zl
    beyond = device_at(1 - zh, y, c, x, zl)
    right = device_at(zh, y, c, lax.rem(x + 1, 4), zl)
    left = device_at(zh, y, c, lax.rem(x + 3, 4), zl)
    across = device_at(zh, y, c, x, 1 - zl)
    order = [lax.rem(x + d, 4) for d in (2, 1, 3, 0)]

    def load(v):
        return pltpu.make_async_copy(trial_ref.at[:, v], buf.at[v], load_sem.at[v])

    for q in (0, 1):
        for dest in order:
            for t in range(2):
                load(dest * 4 + 2 * t + q).start()

    ao_peers = [(lax.axis_index("grid"), lax.rem(a + d, 8)) for d in range(1, 8)]
    grid_peers = [
        (device_at(zh, lax.rem(y + d, 4), c if same else 1 - c, x, zl), 0 if same else 1, slot)
        for d, slot in ((0, 0), (1, 1), (3, 2), (2, 3))
        for same in (True, False)
        if d or not same
    ]
    greet(ao_peers + [peer for peer, _, _ in grid_peers] + [beyond])

    xs = [[x00, x01, x02, x03], [x10, x11, x12, x13]]
    gx = GatherY(x00, lambda i, slot: xs[i][slot], 0, 4, 0, gsend, grecv, (pl.ds(0, SIG),))
    for b in range(4):
        for n in range(SIG):
            x00[b, n] = x_ref[b, :, n * BLK : (n + 1) * BLK].T
    gx.start_first()
    gx.start_second()

    def split(src):
        def some(k, _):
            k = pl.ds(pl.multiple_of(k * 256, 256), 256)
            both = src[k].astype(F32)
            w[k, :NOCC] = both[:, 0, :].astype(BF16)
            w[k, NOCC:] = both[:, 1, :].astype(BF16)
            return 0

        lax.fori_loop(0, w.shape[0] // 256, some, 0)

    zero = jnp.zeros((BLK, BLK), BF16)
    for b in range(4):
        for n in range(SIG):
            xpad[b, n] = x_ref[b, :, n * BLK : (n + 1) * BLK]
        xpad[b, SIG] = zero
    nloc = xloc.shape[1] // BLK
    for b in range(4):
        for l in range(nloc):
            xloc[b * BLK : (b + 1) * BLK, l * BLK : (l + 1) * BLK] = xpad[b, inv_ref[b, a * nloc + l]]

    split(occ_ref)
    od[...] = jnp.dot(xloc[...], w[...], preferred_element_type=F32)
    osum = [
        remote(osend, orecv, d - 1, od.at[rows_of(lax.rem(a + d, 8) * 64, 64)], orec.at[d - 1], ao_peers[d - 1])
        for d in range(1, 8)
    ]
    for copy in osum:
        copy.start()

    es = [e0, e1]
    ge = [
        GatherY(es[q].at[0, 0], lambda i, slot, q=q: es[q].at[i, slot], 0, 4, 10 + 10 * q, gsend, grecv)
        for q in (0, 1)
    ]
    tables = [
        remote(gsend, grecv, 30 + n, place_ref, places.at[i, slot], peer)
        for n, (peer, i, slot) in enumerate(grid_peers)
    ]
    for copy in tables:
        copy.start()
    places[0, 0] = place_ref[...]
    for i in range(2):
        for slot in range(4):
            for b in range(4):
                xs[i][slot][b, SIG] = zero

    def densities(dest, q, store):
        def one(t, _):
            v = dest * 4 + 2 * t + q
            load(v).wait()
            split(buf.at[v])
            store(
                pl.ds(pl.multiple_of(t * 256, 256), 256),
                jnp.dot(xloc[...], w[...], preferred_element_type=F32),
            )
            return 0

        lax.fori_loop(0, 2, one, 0)

    lo, hi = pl.ds(0, 256), pl.ds(256, 256)
    halves = (lo, hi)
    sides = (right, left)
    to_opp = [
        [remote(send, recv, 2 * q + k, opp.at[q, halves[k]], rec1.at[q, halves[k]], sides[k]) for k in (0, 1)]
        for q in (0, 1)
    ]
    to_side = [
        [
            [
                remote(send, recv, 4 + 4 * q + 2 * k + h, part.at[k, q, halves[h]], rec2.at[k, q, halves[h]], sides[k])
                for h in (0, 1)
            ]
            for k in (0, 1)
        ]
        for q in (0, 1)
    ]
    to_pair = [remote(send, recv, 12 + q, zsend.at[q], zrec.at[q], across) for q in (0, 1)]

    def dens_opp(q):
        def store(cols, value):
            opp[q, :, cols] = value.astype(BF16)

        densities(order[0], q, store)
        for copy in to_opp[q]:
            copy.start()

    def dens_side(k, q):
        def store(cols, value):
            own[q, halves[k], cols] = value[256 * k : 256 * k + 256]
            part[k, q, halves[1 - k], cols] = value[256 - 256 * k : 512 - 256 * k].astype(BF16)

        densities(order[1 + k], q, store)
        to_side[q][k][1 - k].start()

    def add_side(k, q):
        to_opp[q][k].wait_recv()

        def some(i, _):
            r = rows_of(256 * k + i * 16, 16)
            part[k, q, r] = (own[q, r] + rec1[q, r].astype(F32)).astype(BF16)
            return 0

        lax.fori_loop(0, 16, some, 0)
        to_side[q][k][k].start()

    def dens_own(q):
        def store(cols, value):
            own[q, :, cols] = value

        densities(order[3], q, store)

    theirs = pl.ds(pl.multiple_of((1 - zl) * 256, 256), 256)
    mine = pl.ds(pl.multiple_of(zl * 256, 256), 256)

    def total(q, r, cols):
        return own[q, r, cols] + rec2[0, q, r, cols].astype(F32) + rec2[1, q, r, cols].astype(F32)

    def to_z(q):
        for k in (0, 1):
            for h in (0, 1):
                to_side[q][k][h].wait_recv()

        def some(i, _):
            r = rows_of(i * 32, 32)
            zsend[q, r] = total(q, r, theirs).astype(BF16)
            return 0

        lax.fori_loop(0, 16, some, 0)
        to_pair[q].start()

    def pair(q):
        to_pair[q].wait_recv()

        def some(i, _):
            r = rows_of(i * 32, 32)
            lg[r] = (total(q, r, mine) + zrec[q, r].astype(F32)).astype(BF16)
            return 0

        lax.fori_loop(0, 16, some, 0)
        for b in range(4):
            rows = pl.ds(b * BLK, BLK)
            ore = og[rows, :NOCC].astype(F32)
            oim = og[rows, NOCC:].astype(F32)
            ww = jnp.concatenate(
                [
                    jnp.concatenate([ore, oim], axis=1),
                    jnp.concatenate([-oim, ore], axis=1),
                ],
                axis=0,
            ).astype(BF16)
            rho = lax.dot_general(
                lg[rows], ww, (((1,), (1,)), ((), ())), preferred_element_type=F32
            )
            m = (rho * jnp.concatenate([kern[b], kern[b]], axis=1)).astype(BF16)
            es[q][0, 0, b] = jnp.dot(m, ww, preferred_element_type=F32).astype(BF16)
        ge[q].start_first()
        ge[q].start_second()

    first = (y * 2 + c) * 6
    GROUP = 3

    def panel(i, slot, q, start, stop, fresh=False):
        def row(n, _):
            lines = []
            for k in range(GROUP):
                r = n * GROUP + k
                block = jnp.where(r < 6, (1 - zh) * 48 + first + r, zh * 48 + first + r - 6)
                lines.append(
                    jnp.concatenate([xs[i][slot][b, table[i, slot, b, block]] for b in range(4)], axis=1)
                )
            value = jnp.dot(
                jnp.concatenate(lines, axis=0), es[q][i, slot].reshape(4 * BLK, 256),
                preferred_element_type=F32,
            ).reshape(GROUP, BLK, 256)
            at = pl.ds(n * GROUP, GROUP)
            acc[q, at] = value if fresh else acc[q, at] + value
            return 0

        lax.fori_loop(start, stop, row, 0)

    over = [
        [remote(hsend, hrecv, 2 * q + n, give.at[q, n], got.at[q, n], beyond) for n in range(2)]
        for q in (0, 1)
    ]

    def middle(q):
        ge[q].spread_opposite()
        ge[q].arrived(4)
        panel(1, 0, q, 0, 4)
        panel(0, 1, q, 0, 4)
        panel(0, 2, q, 0, 4)
        ge[q].arrived(7, 8)
        panel(1, 1, q, 0, 4)
        panel(1, 2, q, 0, 4)
        panel(0, 3, q, 0, 4)

    def last(q):
        ge[q].arrived(9)
        for n in (0, 1):
            panel(1, 3, q, n, n + 1)
            give[q, n] = acc[q, 3 * n : 3 * n + 3].astype(BF16)
            over[q][n].start()
        panel(1, 3, q, 2, 4)

    def finish(q):
        for r in range(6):
            if r % 3 == 0:
                over[q][r // 3].wait_recv()
            for k in range(2):
                cols = slice(k * 128, k * 128 + 128)
                out_ref[q, r * BLK : (r + 1) * BLK, k, :] = acc[q, 6 + r, :, cols] + got[
                    q, r // 3, r % 3, :, cols
                ].astype(F32)

    dens_opp(0)
    dens_side(0, 0)
    for copy in osum:
        copy.wait_recv()
    mine64 = rows_of(a * 64, 64)
    og[mine64] = (od[mine64] + sum(orec[n] for n in range(7))).astype(BF16)
    ogat = [
        remote(osend, orecv, 7 + d - 1, og.at[mine64], og.at[mine64], ao_peers[d - 1])
        for d in range(1, 8)
    ]
    for copy in ogat:
        copy.start()
    add_side(0, 0)
    dens_side(1, 0)
    add_side(1, 0)
    dens_own(0)
    dens_opp(1)
    gx.forward()
    dens_side(0, 1)
    to_z(0)
    dens_side(1, 1)
    add_side(0, 1)
    add_side(1, 1)

    def spread_row(row):
        return jnp.broadcast_to(row, (BLK, BLK))

    for b in range(4):
        square = None
        for k in range(3):
            along = spread_row(coords_ref[k, b : b + 1, :])
            differ = along.T - along
            square = differ * differ if square is None else square + differ * differ
        quad = spread_row(weights_ref[b : b + 1, :])
        kern[b] = quad.T * quad / jnp.sqrt(square + 0.25)
    for copy in tables + ogat:
        copy.wait_recv()
    fill = pltpu.make_async_copy(places, table, local)
    fill.start()
    pair(0)
    fill.wait()
    dens_own(1)
    gx.spread()
    panel(0, 0, 0, 0, 4, fresh=True)
    ge[0].forward()
    ge[0].spread()
    to_z(1)
    gx.spread_opposite()
    gx.arrived(4, 7, 8)
    pair(1)
    middle(0)
    ge[1].forward()
    ge[1].spread()
    gx.arrived(9)
    last(0)
    panel(0, 0, 1, 0, 4, fresh=True)
    middle(1)
    last(1)
    finish(0)
    finish(1)
    for gather in [gx] + ge:
        gather.sent()
    for q in (0, 1):
        for copy in to_opp[q] + to_side[q][0] + to_side[q][1] + over[q] + [to_pair[q]]:
            copy.wait_send()
    for copy in tables + ogat + osum:
        copy.wait_send()


def exchange_step(inv, trial, colloc, occupied, coords, weights):
    rows = trial.shape[0]
    hbm = pl.BlockSpec(memory_space=pl.ANY)
    vmem = pl.BlockSpec(memory_space=pltpu.VMEM)
    smem = pl.BlockSpec(memory_space=pltpu.SMEM)
    return pl.pallas_call(
        main_kernel,
        out_shape=jax.ShapeDtypeStruct((2, 6 * BLK, 2, NOCC), F32),
        in_specs=[smem, hbm, vmem, vmem, vmem, vmem, vmem],
        out_specs=vmem,
        scratch_shapes=[
            *[pltpu.VMEM((4, SIG + 1, BLK, BLK), BF16)] * 8,
            pltpu.VMEM((4, SIG + 1, BLK, BLK), BF16),
            pltpu.VMEM((2, 4, 4, BLK, 256), BF16),
            pltpu.VMEM((2, 4, 4, BLK, 256), BF16),
            pltpu.VMEM((2, 4) + inv.shape, jnp.int32),
            pltpu.SMEM((2, 4) + inv.shape, jnp.int32),
            pltpu.VMEM((4, BLK, BLK), F32),
            pltpu.VMEM((2, 12, BLK, 256), F32),
            pltpu.VMEM((2, 2, 3, BLK, 256), BF16),
            pltpu.VMEM((2, 2, 3, BLK, 256), BF16),
            pltpu.VMEM((16, rows, 2, NOCC), BF16),
            pltpu.VMEM((rows, 256), BF16),
            pltpu.VMEM((ROWS, rows), BF16),
            pltpu.VMEM((2, ROWS, 512), BF16),
            pltpu.VMEM((2, 2, ROWS, 512), BF16),
            pltpu.VMEM((2, ROWS, 512), F32),
            pltpu.VMEM((2, ROWS, 512), BF16),
            pltpu.VMEM((2, 2, ROWS, 512), BF16),
            pltpu.VMEM((2, ROWS, 256), BF16),
            pltpu.VMEM((2, ROWS, 256), BF16),
            pltpu.VMEM((ROWS, 256), BF16),
            pltpu.VMEM((ROWS, 2 * NOCC), F32),
            pltpu.VMEM((7, ROWS // 8, 2 * NOCC), F32),
            pltpu.VMEM((ROWS, 2 * NOCC), BF16),
            pltpu.SemaphoreType.DMA((16,)),
            pltpu.SemaphoreType.DMA((14,)),
            pltpu.SemaphoreType.DMA((14,)),
            pltpu.SemaphoreType.DMA((14,)),
            pltpu.SemaphoreType.DMA((14,)),
            pltpu.SemaphoreType.DMA((37,)),
            pltpu.SemaphoreType.DMA((37,)),
            pltpu.SemaphoreType.DMA((4,)),
            pltpu.SemaphoreType.DMA((4,)),
            pltpu.SemaphoreType.DMA,
        ],
        compiler_params=pltpu.CompilerParams(
            vmem_limit_bytes=63 << 20, collective_id=0, has_side_effects=True
        ),
        name="exchange_step",
    )(inv, trial, colloc, occupied, inv, coords, weights)


def place_of(ids, wanted):
    hit = ids[..., None, :] == wanted[..., :, None]
    where = jnp.arange(SIG, dtype=jnp.int32)
    return SIG + jnp.sum(jnp.where(hit, where - SIG, 0), axis=-1).astype(jnp.int32)


def on_device(trial, occupied, colloc, blocks, coords, weights):
    nblk = trial.shape[0] // BLK * lax.axis_size("ao")
    inv = place_of(blocks, jnp.arange(nblk, dtype=jnp.int32))
    inv = jnp.pad(inv, ((0, 4), (0, BLK - nblk)))
    return exchange_step(inv, trial, colloc, occupied, coords.transpose(1, 0, 2), weights)


def solution(mesh):
    in_specs = (
        P("ao", None, None, None),
        P("ao", None, None),
        P("grid", None, None),
        P("grid", None),
        P("grid", None, None),
        P("grid", None),
    )
    out_specs = P("ao", "grid", None, None)
    return jax.shard_map(
        on_device, mesh=mesh, in_specs=in_specs, out_specs=out_specs, check_vma=False
    )
```
